32 devices in a mesh: sp: 16 (over z, y, x), pb: 2 (over core).
Axes of the slice: x: 2, y: 2, z: 4, core: 2. Of those that a mesh axis runs over, the one named last changes fastest.
Arguments:
- amplitudes: bfloat16 [40, 1024, 1024], P('pb', 'sp'), may hold values from -6 to 6
- virtuals: bfloat16 [1400, 1024], replicated, may hold values from -0.375 to 0.375
- energies: float32 [1024], replicated, may hold values from 0.02 to 0.2
- integrals: bfloat16 [2048, 2048], P('sp'), may hold values from -0.125 to 0.125
- screened: int32 [16, 16], P('sp'), may hold values from 0 to 15, as said below
- counts: int32 [16], P('sp'), may hold values from 1 to 16, 128 in all
- offsets: int32 [2, 16], replicated, may hold values from 0 to 1384
- coupling: bfloat16 [40, 40], P('pb'), may hold values from -1 to 1
Outputs:
- residual: bfloat16 [40, 1024, 1024], P('pb', 'sp')
The draws below stay inside these ranges and needn't reach their ends.
Inputs may be any that keep to these rules, and one draw needn't show every extreme that they name: `screened`: each row names 16 different blocks.
All inputs are finite; a program needn't handle non-finite values. No bound on the sum of `counts` on one device may be relied on, other than what follows from the above.
Results may differ from the reference program's by a relative error of at most 0.01.
Values may be sent and summed in bfloat16 or wider, within the bound.
No kernel may reach another device: no remote copies, remote signals or barrier semaphores. Data moves between devices by JAX's collectives and lax.ppermute only.
A program may use at most 64 MiB of HBM per device.

```python
import math
import jax
import jax.numpy as jnp
import numpy as np
from jax import lax

NAO = 1400
NEXT = 1024
SHELL_ROW = 8
SHELL_COL = 16
KSCR = 16
NPAIR = 40
NBLK = 16


def draw_screened(key, part):
    keys = jax.random.split(jax.random.fold_in(key, 7), NBLK)
    rows = jax.vmap(lambda single: jax.random.permutation(single, NBLK)[:KSCR])(keys)
    return rows.astype(jnp.int32)


def set_ends(drawn, key, smallest, top_value):
    dims = drawn.shape
    index_at = [jax.random.randint(jax.random.fold_in(key, axis), (), 0, dims[axis]) for axis in range(len(dims))]
    drawn = drawn.at[tuple(index_at)].set(smallest)
    longest = dims.index(max(dims))
    index_at[longest] = (index_at[longest] + 1) % dims[longest]
    return drawn.at[tuple(index_at)].set(top_value)


def steps_of(own_key, dims, pieces, low, largest):
    gain, own = 1.0, jax.random.fold_in(own_key, 6)
    for axis_at, shards_of in pieces:
        heights = jnp.exp(jax.random.uniform(jax.random.fold_in(own, axis_at), (shards_of,), jnp.float32, low / len(pieces), largest / len(pieces)))
        gain = gain * jnp.repeat(heights, dims[axis_at] // shards_of).reshape([-1 if axis == axis_at else 1 for axis in range(len(dims))])
    return gain


def length_profile(count, total, reach, lean):
    weights = [(1 << 20) // math.isqrt(rank ** lean) + 1 for rank in range(2, count + 1)]
    spare, given = total - reach - (count - 1), [1] * (count - 1)
    while spare > 0:
        candidates = [i for i in range(count - 1) if given[i] < reach]
        mass, left = sum([weights[i] for i in candidates]), spare
        for i in candidates:
            addition = min(reach - given[i], max(1, left * weights[i] // mass), spare)
            given[i] = given[i] + addition
            spare = spare - addition
    return np.array([reach] + given)


def ragged_sizes(rng, amount, total, bound, skew):
    if amount == 2:
        one = jax.random.randint(rng, (), max(1, total - bound), min(bound, total - 1) + 1)
        return jnp.stack([one, total - one])
    tallies = jnp.asarray(length_profile(amount, total, bound, skew), jnp.int32)
    couples = (amount - 1) // 2
    donor, sink = tallies[1:1 + 2 * couples:2], tallies[2:2 + 2 * couples:2]
    margin = jnp.minimum(donor - 1, bound - sink)
    passed = jax.random.randint(jax.random.fold_in(rng, 1), (couples,), 0, 1 << 20) % (margin + 1)
    tallies = tallies.at[1:1 + 2 * couples:2].set(donor - passed).at[2:2 + 2 * couples:2].set(sink + passed)
    return tallies[jax.random.permutation(jax.random.fold_in(rng, 2), amount)]


def bell_draw(key, shape, scale, most, cuts=(), kind=jnp.bfloat16):
    result = scale * jax.random.normal(key, shape, jnp.float32)
    if cuts:
        result = result * steps_of(key, shape, cuts, -0.22, 0.18)
    return jnp.clip(result, -most, most).astype(kind)


def setup_inputs(seed: int = 0) -> dict:
    streams_of = jax.random.split(jax.random.key(seed), 9)
    return {
        "amplitudes": bell_draw(streams_of[0], (NPAIR, NEXT, NEXT), 1.0, 6.0, ((0, 2), (1, 16))),
        "virtuals": bell_draw(streams_of[1], (NAO, NEXT), 300 ** -0.5, 0.375),
        "energies": jnp.clip(jnp.exp(jax.random.uniform(streams_of[2], (NEXT,), jnp.float32, math.log(0.02), math.log(0.2))), 0.02, 0.2),
        "integrals": bell_draw(streams_of[3], (NBLK * SHELL_ROW * SHELL_COL, KSCR * SHELL_ROW * SHELL_COL), (KSCR * SHELL_ROW * SHELL_COL) ** -0.5, 0.125, ((0, 16),)),
        "screened": draw_screened(jax.random.fold_in(streams_of[8], 71), 0),
        "counts": ragged_sizes(streams_of[5], NBLK, NBLK * KSCR // 2, KSCR, 2).astype(jnp.int32),
        "offsets": set_ends(jax.random.randint(streams_of[6], (2, NBLK), 0, NAO - SHELL_COL + 1), jax.random.fold_in(streams_of[6], 1), 0, NAO - SHELL_COL).astype(jnp.int32),
        "coupling": bell_draw(streams_of[7], (NPAIR, NPAIR), NPAIR ** -0.5, 1.0, ((0, 2),)),
    }


def reference(amplitudes, virtuals, energies, integrals, screened, counts, offsets, coupling):
    width = SHELL_ROW * SHELL_COL
    rows = offsets[0][:, None] + jnp.arange(SHELL_ROW, dtype=jnp.int32)[None, :]
    cols = offsets[1][:, None] + jnp.arange(SHELL_COL, dtype=jnp.int32)[None, :]
    left = virtuals[rows].astype(jnp.float32)
    right = virtuals[cols].astype(jnp.float32)

    def back(amp):
        half = jnp.dot(amp, virtuals.T, preferred_element_type=jnp.float32).astype(jnp.bfloat16)
        half = lax.optimization_barrier(half).astype(jnp.float32)
        picked = half[:, cols]
        blocks = jnp.einsum('bia,abs->bis', left, picked)
        return blocks.reshape(NBLK, width).astype(jnp.bfloat16)

    ao = lax.map(back, amplitudes)
    live = (jnp.arange(KSCR, dtype=jnp.int32)[None, :] < counts[:, None]).astype(jnp.float32)
    chosen = ao[:, screened, :].astype(jnp.float32) * live[None, :, :, None]
    slab = integrals.astype(jnp.float32).reshape(NBLK, width, KSCR, width)
    raw = jnp.einsum('jrkc,pjkc->pjr', slab, chosen).astype(jnp.bfloat16)
    mixed = jnp.einsum('pq,qjr->pjr', coupling.astype(jnp.float32), raw.astype(jnp.float32)).astype(jnp.bfloat16)
    diag = energies[:, None] + energies[None, :]

    def forward(pair):
        kmix, amp = pair
        square = kmix.astype(jnp.float32).reshape(NBLK, SHELL_ROW, SHELL_COL)
        upper = jnp.einsum('bia,bis->abs', left, square).astype(jnp.bfloat16)
        upper = lax.optimization_barrier(upper).astype(jnp.float32)
        inner = jnp.einsum('abs,bsn->an', upper, right)
        return (inner + diag * amp.astype(jnp.float32)).astype(jnp.bfloat16)

    return lax.map(forward, (mixed, amplitudes))
```

```python
import functools

import jax
import jax.numpy as jnp
from jax import lax
from jax.experimental import pallas as pl
from jax.experimental.pallas import tpu as pltpu
from jax.sharding import PartitionSpec as P

SHELL_ROW = 8
SHELL_COL = 16
WIDTH = SHELL_ROW * SHELL_COL
GROUP = 2
SUB = 16
RIGHT_WIN = 32
LEFT_WIN = 16
LANES = 128
F32 = jnp.float32
BF16 = jnp.bfloat16
VMEM_LIMIT = 60 * 1024 * 1024


def iota(shape, dim):
    return lax.broadcasted_iota(jnp.int32, shape, dim)


def dot(a, b):
    return jnp.dot(a, b, preferred_element_type=F32)


def dot_t(a, b):
    return lax.dot_general(a, b, (((1,), (1,)), ((), ())), preferred_element_type=F32)


def chunk_of(pairs):
    return max(c for c in range(1, 6) if pairs % c == 0)


def window(low, size, nao):
    base = jnp.minimum(low // 8 * 8, nao - size)
    return pl.multiple_of(base, 8)


def back_kernel(
    nblk, ext_rows, offs, amp, virt, out, right_out, left_out, right_win, left_win, acc, sems
):
    nao, next_ = virt.shape
    first = lax.axis_index("sp") * ext_rows

    @pl.when(pl.program_id(0) == 0)
    def _():
        lane_base = pl.multiple_of(first // LANES * LANES, LANES)
        shift = first - lane_base
        copies = []
        for b in range(nblk):
            base = window(offs[1, b], RIGHT_WIN, nao)
            copies.append(
                pltpu.make_async_copy(
                    virt.at[pl.ds(base, RIGHT_WIN), :], right_win.at[b], sems.at[0, b]
                )
            )
            base = window(offs[0, b], LEFT_WIN, nao)
            copies.append(
                pltpu.make_async_copy(
                    virt.at[pl.ds(base, LEFT_WIN), pl.ds(lane_base, LANES)],
                    left_win.at[b],
                    sems.at[1, b],
                )
            )
        for copy in copies:
            copy.start()
        for copy in copies:
            copy.wait()
        half_sub = SUB // 2
        for g in range(nblk // half_sub):
            rows, cols = half_sub * SHELL_COL, half_sub * RIGHT_WIN
            row, col = iota((SHELL_COL, cols), 0), iota((SHELL_COL, cols), 1)
            parts = []
            for t in range(half_sub):
                low = offs[1, g * half_sub + t]
                delta = low - window(low, RIGHT_WIN, nao) + t * RIGHT_WIN
                parts.append(jnp.where(col == row + delta, 1.0, 0.0))
            pick = jnp.concatenate(parts, axis=0).astype(BF16)
            win = right_win[g * half_sub : (g + 1) * half_sub].reshape(cols, next_)
            right_out[g * rows : (g + 1) * rows, :] = dot(pick, win).astype(BF16)
        lane_pick = jnp.where(
            iota((LANES, ext_rows), 0) == iota((LANES, ext_rows), 1) + shift, 1.0, 0.0
        ).astype(BF16)
        for g in range(nblk // SUB):
            rows, cols = SUB * SHELL_ROW, SUB * LEFT_WIN
            row, col = iota((SHELL_ROW, cols), 0), iota((SHELL_ROW, cols), 1)
            parts = []
            for t in range(SUB):
                low = offs[0, g * SUB + t]
                delta = low - window(low, LEFT_WIN, nao) + t * LEFT_WIN
                parts.append(jnp.where(col == row + delta, 1.0, 0.0))
            pick = jnp.concatenate(parts, axis=0).astype(BF16)
            win = left_win[g * SUB : (g + 1) * SUB].reshape(cols, LANES)
            wide = dot(pick, win).astype(BF16)
            left_out[g * rows : (g + 1) * rows, :] = dot(wide, lane_pick).astype(BF16)

    chunk = amp.shape[0]
    half = dot_t(amp[...].reshape(chunk * ext_rows, next_), right_out[...]).astype(BF16)
    span = SUB * SHELL_COL
    block_of = iota((SHELL_ROW, span), 1) // SHELL_COL
    for q in range(chunk):
        own = half[q * ext_rows : (q + 1) * ext_rows]
        for g in range(nblk // SUB):
            left = left_out[g * SUB * SHELL_ROW : (g + 1) * SUB * SHELL_ROW, :]
            full = dot(left, own[:, g * span : (g + 1) * span])
            kept = full[:SHELL_ROW]
            for t in range(1, SUB):
                kept = jnp.where(
                    block_of == t, full[t * SHELL_ROW : (t + 1) * SHELL_ROW], kept
                )
            acc[q * SHELL_ROW : (q + 1) * SHELL_ROW, g * span : (g + 1) * span] = kept
    done = acc[...].astype(BF16)
    for copy in range(out.shape[0]):
        out[copy, 0] = done


def raw_kernel(slots, lists, live, got, *rest):
    slabs, out = rest[:-1], rest[-1]
    total = got[0].astype(F32)
    for src in range(1, got.shape[0]):
        total = total + got[src].astype(F32)
    ao = total.astype(BF16)
    rows, span = ao.shape
    cols = slots * SHELL_COL
    lane = iota((1, cols), 1)
    chosen = []
    for t in range(len(slabs)):
        target = jnp.full((1, cols), -1, jnp.int32)
        for k in range(slots):
            block = jnp.where(k < live[t, 0], lists[t, k], -nblk_guard(span))
            target = jnp.where(
                lane // SHELL_COL == k, block * SHELL_COL + lane % SHELL_COL, target
            )
        pick = jnp.where(iota((span, cols), 0) == target, 1.0, 0.0).astype(BF16)
        chosen.append(dot(ao, pick).astype(BF16))
    wide = slots * WIDTH
    down, across = iota((cols, wide), 0), iota((cols, wide), 1)
    spread = jnp.where(
        (down // SHELL_COL == across // WIDTH) & (down % SHELL_COL == across % SHELL_COL),
        1.0,
        0.0,
    ).astype(BF16)
    mask = iota((rows, wide), 0) % SHELL_ROW == iota((rows, wide), 1) % WIDTH // SHELL_COL
    pieces = []
    for t, slab in enumerate(slabs):
        laid = jnp.where(mask, dot(chosen[t], spread), 0.0).astype(BF16)
        raw = dot_t(laid, slab[...])
        pieces.append(jnp.sum(raw.reshape(rows // SHELL_ROW, SHELL_ROW, WIDTH), axis=1))
    done = jnp.concatenate(pieces, axis=0).astype(BF16)
    for copy in range(out.shape[0]):
        out[copy] = done


def nblk_guard(span):
    return span


def residual_kernel(
    groups, halves, nblk, ext_rows, raws, coupling, left, right, energies, amp, out, mixed, own_e
):
    pairs = coupling.shape[0]
    rows = raws.shape[1]
    each = rows // GROUP
    next_ = right.shape[1]

    @pl.when(pl.program_id(0) == 0)
    def _():
        first = lax.axis_index("sp") * ext_rows
        wide_e = energies[...]
        pick = iota((ext_rows, next_), 1) == iota((ext_rows, next_), 0) + first
        own_e[...] = jnp.sum(jnp.where(pick, wide_e, 0.0), axis=1, keepdims=True)
        couple = coupling[...]
        total = [None] * GROUP
        for member in range(GROUP):
            for h in range(halves):
                data = jnp.concatenate(
                    [raws[(g * GROUP + member) * halves + h] for g in range(groups)], axis=1
                )
                down, across = iota((couple.shape[1], rows), 0), iota((couple.shape[1], rows), 1)
                source = h * pairs + member * each + across % each
                for j in range(GROUP):
                    turn = (j - member) % GROUP
                    here = (down == source) & (across // each == turn)
                    weights = dot(couple, jnp.where(here, 1.0, 0.0).astype(BF16)).astype(BF16)
                    term = dot(weights, data)
                    total[j] = term if total[j] is None else total[j] + term
        for j in range(GROUP):
            done = total[j].astype(BF16).astype(F32)
            for c in range(mixed.shape[0]):
                mixed[c, j] = done[c * mixed.shape[2] : (c + 1) * mixed.shape[2]]

    chunk = amp.shape[0]
    span = SUB * SHELL_COL
    mask = iota((SHELL_ROW, WIDTH), 0) == iota((SHELL_ROW, WIDTH), 1) // SHELL_COL
    tile = jnp.where(
        iota((WIDTH, span), 0) % SHELL_COL == iota((WIDTH, span), 1) % SHELL_COL, 1.0, 0.0
    ).astype(BF16)
    high = SUB * SHELL_ROW
    diagonal = iota((high, span), 0) // SHELL_ROW == iota((high, span), 1) // SHELL_COL
    step = pl.program_id(0)
    uppers = []
    for q in range(chunk):
        columns = []
        for g in range(nblk // SUB):
            stack = []
            for t in range(SUB):
                b = g * SUB + t
                lanes = pl.ds(b // GROUP * WIDTH, WIDTH)
                row = mixed[step, b % GROUP, q : q + 1, lanes]
                stack.append(jnp.where(mask, jnp.broadcast_to(row, (SHELL_ROW, WIDTH)), 0.0))
            flat = jnp.concatenate(stack, axis=0).astype(BF16)
            square = jnp.where(diagonal, dot(flat, tile), 0.0).astype(BF16)
            part = left[g * high : (g + 1) * high, :]
            columns.append(
                lax.dot_general(part, square, (((0,), (0,)), ((), ())), preferred_element_type=F32)
            )
        uppers.append(jnp.concatenate(columns, axis=1).astype(BF16))
    upper = jnp.concatenate(uppers, axis=0)
    inner = dot(upper, right[...]).reshape(chunk, ext_rows, next_)
    diag = own_e[...] + energies[...]
    out[...] = (inner + diag[None] * amp[...].astype(F32)).astype(BF16)


def shards(amplitudes, virtuals, energies, integrals, screened, counts, offsets, coupling):
    pairs, ext_rows, next_ = amplitudes.shape
    nblk = offsets.shape[1]
    n = lax.axis_size("sp")
    halves = lax.axis_size("pb")
    slots = screened.shape[1]
    span = nblk * SHELL_COL
    each = pairs // GROUP
    rows = each * SHELL_ROW

    facts = jnp.concatenate([screened, counts[:, None]], axis=1)
    slabs, lists = [integrals], [facts]
    for turn in range(1, GROUP):
        ring = [
            (i // GROUP * GROUP + (i + turn) % GROUP, i) for i in range(n)
        ]
        slabs.append(lax.ppermute(integrals, "sp", ring))
        lists.append(lax.ppermute(facts, "sp", ring))
    facts = jnp.concatenate(lists, axis=0)

    chunk = chunk_of(each)
    smem = pl.BlockSpec(memory_space=pltpu.SMEM)
    vmem = pl.BlockSpec(memory_space=pltpu.VMEM)
    params = pltpu.CompilerParams(
        dimension_semantics=("arbitrary",), vmem_limit_bytes=VMEM_LIMIT
    )
    per = each // chunk
    partial, right, left = pl.pallas_call(
        functools.partial(back_kernel, nblk, ext_rows),
        grid=(pairs // chunk,),
        in_specs=[
            smem,
            pl.BlockSpec((chunk, ext_rows, next_), lambda c: (c, 0, 0)),
            pl.BlockSpec(memory_space=pltpu.HBM),
        ],
        out_specs=[
            pl.BlockSpec(
                (n // GROUP, 1, chunk * SHELL_ROW, span), lambda c: (0, c // per, c % per, 0)
            ),
            pl.BlockSpec((span, next_), lambda c: (0, 0)),
            pl.BlockSpec((nblk * SHELL_ROW, ext_rows), lambda c: (0, 0)),
        ],
        out_shape=[
            jax.ShapeDtypeStruct((n // GROUP, GROUP, rows, span), BF16),
            jax.ShapeDtypeStruct((span, next_), BF16),
            jax.ShapeDtypeStruct((nblk * SHELL_ROW, ext_rows), BF16),
        ],
        scratch_shapes=[
            pltpu.VMEM((nblk, RIGHT_WIN, next_), BF16),
            pltpu.VMEM((nblk, LEFT_WIN, LANES), BF16),
            pltpu.VMEM((chunk * SHELL_ROW, span), F32),
            pltpu.SemaphoreType.DMA((2, nblk)),
        ],
        compiler_params=params,
        name="back",
    )(offsets, amplitudes, virtuals)

    got = lax.all_to_all(partial.reshape(n, rows, span), "sp", 0, 0, tiled=True)

    raw = pl.pallas_call(
        functools.partial(raw_kernel, slots),
        in_specs=[smem, smem] + [vmem] * (1 + GROUP),
        out_specs=vmem,
        out_shape=jax.ShapeDtypeStruct((n * halves, GROUP * each, WIDTH), BF16),
        compiler_params=pltpu.CompilerParams(vmem_limit_bytes=VMEM_LIMIT),
        name="raw",
    )(facts[:, :slots], facts[:, slots:], got, *slabs)

    raws = lax.all_to_all(raw, ("sp", "pb"), 0, 0, tiled=True)

    return pl.pallas_call(
        functools.partial(residual_kernel, n // GROUP, halves, nblk, ext_rows),
        grid=(pairs // chunk,),
        in_specs=[
            pl.BlockSpec(raws.shape, lambda c: (0, 0, 0)),
            pl.BlockSpec(coupling.shape, lambda c: (0, 0)),
            pl.BlockSpec(left.shape, lambda c: (0, 0)),
            pl.BlockSpec(right.shape, lambda c: (0, 0)),
            pl.BlockSpec((1, next_), lambda c: (0, 0)),
            pl.BlockSpec((chunk, ext_rows, next_), lambda c: (c, 0, 0)),
        ],
        out_specs=pl.BlockSpec((chunk, ext_rows, next_), lambda c: (c, 0, 0)),
        out_shape=jax.ShapeDtypeStruct(amplitudes.shape, BF16),
        scratch_shapes=[
            pltpu.VMEM((pairs // chunk, GROUP, chunk, n // GROUP * WIDTH), F32),
            pltpu.VMEM((ext_rows, 1), F32),
        ],
        compiler_params=params,
        name="residual",
    )(raws, coupling, left, right, energies[None], amplitudes)


def solution(mesh):
    return jax.shard_map(
        shards,
        mesh=mesh,
        in_specs=(
            P("pb", "sp", None),
            P(),
            P(),
            P("sp", None),
            P("sp", None),
            P("sp"),
            P(),
            P("pb", None),
        ),
        out_specs=P("pb", "sp", None),
        check_vma=False,
    )
```

```python
import functools

import jax
import jax.numpy as jnp
from jax import lax
from jax.experimental import pallas as pl
from jax.experimental.pallas import tpu as pltpu
from jax.sharding import PartitionSpec as P

SHELL_ROW = 8
SHELL_COL = 16
WIDTH = SHELL_ROW * SHELL_COL
GROUP = 2
SUB = 16
RIGHT_WIN = 32
LEFT_WIN = 16
LANES = 128
F32 = jnp.float32
BF16 = jnp.bfloat16


def iota(shape, dim):
    return lax.broadcasted_iota(jnp.int32, shape, dim)


def dot(a, b):
    return jnp.dot(a, b, preferred_element_type=F32)


def dot_t(a, b):
    return lax.dot_general(a, b, (((1,), (1,)), ((), ())), preferred_element_type=F32)


def chunk_of(pairs):
    return max(c for c in range(1, 6) if pairs % c == 0)


def window(low, size, nao):
    base = jnp.minimum(low // 8 * 8, nao - size)
    return pl.multiple_of(base, 8)


def back_kernel(
    nblk, ext_rows, offs, amp, virt, out, right_out, left_out, right_win, left_win, acc, sems
):
    nao, next_ = virt.shape
    first = lax.axis_index("sp") * ext_rows

    @pl.when(pl.program_id(0) == 0)
    def _():
        lane_base = pl.multiple_of(first // LANES * LANES, LANES)
        shift = first - lane_base
        copies = []
        for b in range(nblk):
            base = window(offs[1, b], RIGHT_WIN, nao)
            copies.append(
                pltpu.make_async_copy(
                    virt.at[pl.ds(base, RIGHT_WIN), :], right_win.at[b], sems.at[0, b]
                )
            )
            base = window(offs[0, b], LEFT_WIN, nao)
            copies.append(
                pltpu.make_async_copy(
                    virt.at[pl.ds(base, LEFT_WIN), pl.ds(lane_base, LANES)],
                    left_win.at[b],
                    sems.at[1, b],
                )
            )
        for copy in copies:
            copy.start()
        for copy in copies:
            copy.wait()
        half_sub = SUB // 2
        for g in range(nblk // half_sub):
            rows, cols = half_sub * SHELL_COL, half_sub * RIGHT_WIN
            row, col = iota((SHELL_COL, cols), 0), iota((SHELL_COL, cols), 1)
            parts = []
            for t in range(half_sub):
                low = offs[1, g * half_sub + t]
                delta = low - window(low, RIGHT_WIN, nao) + t * RIGHT_WIN
                parts.append(jnp.where(col == row + delta, 1.0, 0.0))
            pick = jnp.concatenate(parts, axis=0).astype(BF16)
            win = right_win[g * half_sub : (g + 1) * half_sub].reshape(cols, next_)
            right_out[g * rows : (g + 1) * rows, :] = dot(pick, win).astype(BF16)
        lane_pick = jnp.where(
            iota((LANES, ext_rows), 0) == iota((LANES, ext_rows), 1) + shift, 1.0, 0.0
        ).astype(BF16)
        for g in range(nblk // SUB):
            rows, cols = SUB * SHELL_ROW, SUB * LEFT_WIN
            row, col = iota((SHELL_ROW, cols), 0), iota((SHELL_ROW, cols), 1)
            parts = []
            for t in range(SUB):
                low = offs[0, g * SUB + t]
                delta = low - window(low, LEFT_WIN, nao) + t * LEFT_WIN
                parts.append(jnp.where(col == row + delta, 1.0, 0.0))
            pick = jnp.concatenate(parts, axis=0).astype(BF16)
            win = left_win[g * SUB : (g + 1) * SUB].reshape(cols, LANES)
            wide = dot(pick, win).astype(BF16)
            left_out[g * rows : (g + 1) * rows, :] = dot(wide, lane_pick).astype(BF16)

    chunk = amp.shape[0]
    half = dot_t(amp[...].reshape(chunk * ext_rows, next_), right_out[...]).astype(BF16)
    span = SUB * SHELL_COL
    block_of = iota((SHELL_ROW, span), 1) // SHELL_COL
    for q in range(chunk):
        own = half[q * ext_rows : (q + 1) * ext_rows]
        for g in range(nblk // SUB):
            left = left_out[g * SUB * SHELL_ROW : (g + 1) * SUB * SHELL_ROW, :]
            full = dot(left, own[:, g * span : (g + 1) * span])
            kept = full[:SHELL_ROW]
            for t in range(1, SUB):
                kept = jnp.where(
                    block_of == t, full[t * SHELL_ROW : (t + 1) * SHELL_ROW], kept
                )
            acc[q * SHELL_ROW : (q + 1) * SHELL_ROW, g * span : (g + 1) * span] = kept
    done = acc[...].astype(BF16)
    for copy in range(out.shape[0]):
        out[copy, 0] = done


def raw_kernel(slots, lists, live, got, *rest):
    slabs, out = rest[:-1], rest[-1]
    total = got[0].astype(F32)
    for src in range(1, got.shape[0]):
        total = total + got[src].astype(F32)
    ao = total.astype(BF16)
    rows, span = ao.shape
    cols = slots * SHELL_COL
    lane = iota((1, cols), 1)
    chosen = []
    for t in range(len(slabs)):
        target = jnp.full((1, cols), -1, jnp.int32)
        for k in range(slots):
            block = jnp.where(k < live[t, 0], lists[t, k], -span)
            target = jnp.where(
                lane // SHELL_COL == k, block * SHELL_COL + lane % SHELL_COL, target
            )
        pick = jnp.where(iota((span, cols), 0) == target, 1.0, 0.0).astype(BF16)
        chosen.append(dot(ao, pick).astype(BF16))
    wide = slots * WIDTH
    down, across = iota((cols, wide), 0), iota((cols, wide), 1)
    spread = jnp.where(
        (down // SHELL_COL == across // WIDTH) & (down % SHELL_COL == across % SHELL_COL),
        1.0,
        0.0,
    ).astype(BF16)
    mask = iota((rows, wide), 0) % SHELL_ROW == iota((rows, wide), 1) % WIDTH // SHELL_COL
    pieces = []
    for t, slab in enumerate(slabs):
        laid = jnp.where(mask, dot(chosen[t], spread), 0.0).astype(BF16)
        raw = dot_t(laid, slab[...])
        pieces.append(jnp.sum(raw.reshape(rows // SHELL_ROW, SHELL_ROW, WIDTH), axis=1))
    done = jnp.concatenate(pieces, axis=0).astype(BF16)
    for copy in range(out.shape[0]):
        out[copy] = done


def residual_kernel(
    groups, halves, nblk, ext_rows, raws, coupling, left, right, energies, amp, out, mixed, own_e
):
    pairs = coupling.shape[0]
    rows = raws.shape[1]
    each = rows // GROUP
    next_ = right.shape[1]

    @pl.when(pl.program_id(0) == 0)
    def _():
        first = lax.axis_index("sp") * ext_rows
        wide_e = energies[...]
        pick = iota((ext_rows, next_), 1) == iota((ext_rows, next_), 0) + first
        own_e[...] = jnp.sum(jnp.where(pick, wide_e, 0.0), axis=1, keepdims=True)
        couple = coupling[...]
        total = [None] * GROUP
        for member in range(GROUP):
            for h in range(halves):
                data = jnp.concatenate(
                    [raws[(g * GROUP + member) * halves + h] for g in range(groups)], axis=1
                )
                down, across = iota((couple.shape[1], rows), 0), iota((couple.shape[1], rows), 1)
                source = h * pairs + member * each + across % each
                for j in range(GROUP):
                    turn = (j - member) % GROUP
                    here = (down == source) & (across // each == turn)
                    weights = dot(couple, jnp.where(here, 1.0, 0.0).astype(BF16)).astype(BF16)
                    term = dot(weights, data)
                    total[j] = term if total[j] is None else total[j] + term
        for j in range(GROUP):
            done = total[j].astype(BF16).astype(F32)
            for c in range(mixed.shape[0]):
                mixed[c, j] = done[c * mixed.shape[2] : (c + 1) * mixed.shape[2]]

    chunk = amp.shape[0]
    span = SUB * SHELL_COL
    mask = iota((SHELL_ROW, WIDTH), 0) == iota((SHELL_ROW, WIDTH), 1) // SHELL_COL
    tile = jnp.where(
        iota((WIDTH, span), 0) % SHELL_COL == iota((WIDTH, span), 1) % SHELL_COL, 1.0, 0.0
    ).astype(BF16)
    high = SUB * SHELL_ROW
    diagonal = iota((high, span), 0) // SHELL_ROW == iota((high, span), 1) // SHELL_COL
    step = pl.program_id(0)
    uppers = []
    for q in range(chunk):
        columns = []
        for g in range(nblk // SUB):
            stack = []
            for t in range(SUB):
                b = g * SUB + t
                lanes = pl.ds(b // GROUP * WIDTH, WIDTH)
                row = mixed[step, b % GROUP, q : q + 1, lanes]
                stack.append(jnp.where(mask, jnp.broadcast_to(row, (SHELL_ROW, WIDTH)), 0.0))
            flat = jnp.concatenate(stack, axis=0).astype(BF16)
            square = jnp.where(diagonal, dot(flat, tile), 0.0).astype(BF16)
            part = left[g * high : (g + 1) * high, :]
            columns.append(
                lax.dot_general(part, square, (((0,), (0,)), ((), ())), preferred_element_type=F32)
            )
        uppers.append(jnp.concatenate(columns, axis=1).astype(BF16))
    upper = jnp.concatenate(uppers, axis=0)
    inner = dot(upper, right[...]).reshape(chunk, ext_rows, next_)
    diag = own_e[...] + energies[...]
    out[...] = (inner + diag[None] * amp[...].astype(F32)).astype(BF16)


def shards(amplitudes, virtuals, energies, integrals, screened, counts, offsets, coupling):
    pairs, ext_rows, next_ = amplitudes.shape
    nblk = offsets.shape[1]
    n = lax.axis_size("sp")
    halves = lax.axis_size("pb")
    slots = screened.shape[1]
    span = nblk * SHELL_COL
    each = pairs // GROUP
    rows = each * SHELL_ROW

    facts = jnp.concatenate([screened, counts[:, None]], axis=1)
    slabs, lists = [integrals], [facts]
    for turn in range(1, GROUP):
        ring = [
            (i // GROUP * GROUP + (i + turn) % GROUP, i) for i in range(n)
        ]
        slabs.append(lax.ppermute(integrals, "sp", ring))
        lists.append(lax.ppermute(facts, "sp", ring))
    facts = jnp.concatenate(lists, axis=0)

    chunk = chunk_of(each)
    smem = pl.BlockSpec(memory_space=pltpu.SMEM)
    vmem = pl.BlockSpec(memory_space=pltpu.VMEM)
    grant = min(60, nblk) * 1024 * 1024
    params = pltpu.CompilerParams(
        dimension_semantics=("arbitrary",), vmem_limit_bytes=grant
    )
    per = each // chunk
    back = pl.pallas_call(
        functools.partial(back_kernel, nblk, ext_rows),
        grid=(pairs // chunk,),
        in_specs=[
            smem,
            pl.BlockSpec((chunk, ext_rows, next_), lambda c: (c, 0, 0)),
            pl.BlockSpec(memory_space=pltpu.HBM),
        ],
        out_specs=[
            pl.BlockSpec(
                (n // GROUP, 1, chunk * SHELL_ROW, span), lambda c: (0, c // per, c % per, 0)
            ),
            pl.BlockSpec((span, next_), lambda c: (0, 0)),
            pl.BlockSpec((nblk * SHELL_ROW, ext_rows), lambda c: (0, 0)),
        ],
        out_shape=[
            jax.ShapeDtypeStruct((n // GROUP, GROUP, rows, span), BF16),
            jax.ShapeDtypeStruct((span, next_), BF16),
            jax.ShapeDtypeStruct((nblk * SHELL_ROW, ext_rows), BF16),
        ],
        scratch_shapes=[
            pltpu.VMEM((nblk, RIGHT_WIN, next_), BF16),
            pltpu.VMEM((nblk, LEFT_WIN, LANES), BF16),
            pltpu.VMEM((chunk * SHELL_ROW, span), F32),
            pltpu.SemaphoreType.DMA((2, nblk)),
        ],
        compiler_params=pltpu.CompilerParams(
            dimension_semantics=("arbitrary",), vmem_limit_bytes=60 * 1024 * 1024
        ),
        name="back",
    )
    partial, right, left = back(offsets, amplitudes, virtuals)

    got = lax.all_to_all(partial.reshape(n, rows, span), "sp", 0, 0, tiled=True)

    raw = pl.pallas_call(
        functools.partial(raw_kernel, slots),
        in_specs=[smem, smem] + [vmem] * (1 + GROUP),
        out_specs=vmem,
        out_shape=jax.ShapeDtypeStruct((n * halves, GROUP * each, WIDTH), BF16),
        compiler_params=pltpu.CompilerParams(vmem_limit_bytes=grant),
        name="raw",
    )(facts[:, :slots], facts[:, slots:], got, *slabs)

    raws = lax.all_to_all(raw, ("sp", "pb"), 0, 0, tiled=True)

    return pl.pallas_call(
        functools.partial(residual_kernel, n // GROUP, halves, nblk, ext_rows),
        grid=(pairs // chunk,),
        in_specs=[
            pl.BlockSpec(raws.shape, lambda c: (0, 0, 0)),
            pl.BlockSpec(coupling.shape, lambda c: (0, 0)),
            pl.BlockSpec(left.shape, lambda c: (0, 0)),
            pl.BlockSpec(right.shape, lambda c: (0, 0)),
            pl.BlockSpec((1, next_), lambda c: (0, 0)),
            pl.BlockSpec((chunk, ext_rows, next_), lambda c: (c, 0, 0)),
        ],
        out_specs=pl.BlockSpec((chunk, ext_rows, next_), lambda c: (c, 0, 0)),
        out_shape=jax.ShapeDtypeStruct(amplitudes.shape, BF16),
        scratch_shapes=[
            pltpu.VMEM((pairs // chunk, GROUP, chunk, n // GROUP * WIDTH), F32),
            pltpu.VMEM((ext_rows, 1), F32),
        ],
        compiler_params=params,
        name="residual",
    )(raws, coupling, left, right, energies[None], amplitudes)


def solution(mesh):
    return jax.shard_map(
        shards,
        mesh=mesh,
        in_specs=(
            P("pb", "sp", None),
            P(),
            P(),
            P("sp", None),
            P("sp", None),
            P("sp"),
            P(),
            P("pb", None),
        ),
        out_specs=P("pb", "sp", None),
        check_vma=False,
    )
```

```python
import functools

import jax
import jax.numpy as jnp
from jax import lax
from jax.experimental import pallas as pl
from jax.experimental.pallas import tpu as pltpu
from jax.sharding import PartitionSpec as P

SHELL_ROW = 8
SHELL_COL = 16
WIDTH = SHELL_ROW * SHELL_COL
SUB = 16
RIGHT_WIN = 32
LEFT_WIN = 16
LANES = 128
PACK = 32
F32 = jnp.float32
BF16 = jnp.bfloat16
VMEM = pl.BlockSpec(memory_space=pltpu.VMEM)
HBM = pl.BlockSpec(memory_space=pltpu.HBM)


def iota(shape, dim):
    return lax.broadcasted_iota(jnp.int32, shape, dim)


def dot(a, b):
    return jnp.dot(a, b, preferred_element_type=F32)


def dot_t(a, b):
    return lax.dot_general(a, b, (((1,), (1,)), ((), ())), preferred_element_type=F32)


def chunk_of(pairs):
    return max(c for c in range(1, 6) if pairs % c == 0)


def window(low, size, nao):
    base = jnp.minimum(low // 8 * 8, nao - size)
    return pl.multiple_of(base, 8)


def picks(offs, which, first, count, shell, size, nao):
    cols = count * size
    row, col = iota((shell, cols), 0), iota((shell, cols), 1)
    parts = []
    for t in range(count):
        low = offs[which, first + t]
        delta = low - window(low, size, nao) + t * size
        parts.append(jnp.where(col == row + delta, 1.0, 0.0))
    return jnp.concatenate(parts, axis=0).astype(BF16)


def back_kernel(
    nblk, chunk, offs_in, lists_in, live, amp, virt, slab, out, right, left, amps, slab_out, pick_out,
    offs, lists, right_win, left_win, acc, sems, amp_sems
):
    pairs, ext_rows, next_ = amp.shape
    nao = virt.shape[0]
    first = lax.axis_index("sp") * ext_rows
    lane_base = pl.multiple_of(first // LANES * LANES, LANES)
    shift = first - lane_base
    rights, lefts, loads = [], [], []
    facts = [
        pltpu.make_async_copy(offs_in, offs, amp_sems.at[pairs // chunk + 1]),
        pltpu.make_async_copy(lists_in, lists, amp_sems.at[pairs // chunk + 2]),
    ]
    for fact in facts:
        fact.start()
    facts[0].wait()
    for b in range(nblk):
        base = window(offs[1, b], RIGHT_WIN, nao)
        rights.append(
            pltpu.make_async_copy(
                virt.at[pl.ds(base, RIGHT_WIN), :], right_win.at[b], sems.at[0, b]
            )
        )
        rights[-1].start()
    for c in range(pairs // chunk):
        span_c = pl.ds(c * chunk, chunk)
        loads.append(pltpu.make_async_copy(amp.at[span_c], amps.at[span_c], amp_sems.at[c]))
    loads[0].start()
    for b in range(nblk):
        base = window(offs[0, b], LEFT_WIN, nao)
        lefts.append(
            pltpu.make_async_copy(
                virt.at[pl.ds(base, LEFT_WIN), pl.ds(lane_base, LANES)],
                left_win.at[b],
                sems.at[1, b],
            )
        )
        lefts[-1].start()
    for load in loads[1:]:
        load.start()
    slab_load = pltpu.make_async_copy(slab, slab_out, amp_sems.at[pairs // chunk])
    slab_load.start()
    half_sub = SUB // 2
    rows, cols = half_sub * SHELL_COL, half_sub * RIGHT_WIN
    for g in range(nblk // half_sub):
        pick = picks(offs, 1, g * half_sub, half_sub, SHELL_COL, RIGHT_WIN, nao)
        for b in range(g * half_sub, (g + 1) * half_sub):
            rights[b].wait()
        win = right_win[g * half_sub : (g + 1) * half_sub].reshape(cols, next_)
        right[g * rows : (g + 1) * rows, :] = dot(pick, win).astype(BF16)
    lane_pick = jnp.where(
        iota((LANES, ext_rows), 0) == iota((LANES, ext_rows), 1) + shift, 1.0, 0.0
    ).astype(BF16)
    high = SUB * SHELL_ROW
    for g in range(nblk // SUB):
        pick = picks(offs, 0, g * SUB, SUB, SHELL_ROW, LEFT_WIN, nao)
        for b in range(g * SUB, (g + 1) * SUB):
            lefts[b].wait()
        win = left_win[g * SUB : (g + 1) * SUB].reshape(SUB * LEFT_WIN, LANES)
        wide = dot(pick, win).astype(BF16)
        left[g * high : (g + 1) * high, :] = dot(wide, lane_pick).astype(BF16)

    span = SUB * SHELL_COL
    block_of = iota((SHELL_ROW, span), 1) // SHELL_COL
    for c in range(pairs // chunk):
        loads[c].wait()
        data = amps[c * chunk : (c + 1) * chunk].reshape(chunk * ext_rows, next_)
        half = dot_t(data, right[...]).astype(BF16)
        for q in range(chunk):
            own = half[q * ext_rows : (q + 1) * ext_rows]
            for g in range(nblk // SUB):
                full = dot(left[g * high : (g + 1) * high, :], own[:, g * span : (g + 1) * span])
                kept = full[:SHELL_ROW]
                for t in range(1, SUB):
                    kept = jnp.where(
                        block_of == t, full[t * SHELL_ROW : (t + 1) * SHELL_ROW], kept
                    )
                acc[:, c * chunk + q, g * span : (g + 1) * span] = kept
    tiles = nblk * SHELL_COL // LANES
    for i in range(SHELL_ROW):
        for t in range(tiles):
            done = acc[i, :, t * LANES : (t + 1) * LANES].astype(BF16)
            for h in range(out.shape[1]):
                out[i * tiles + t, h] = done
    for fact in facts[1:]:
        fact.wait()
    slots = lists.shape[1]
    whole, cols = nblk * SHELL_COL, slots * SHELL_COL
    lane = iota((1, cols), 1)
    target = jnp.full((1, cols), -1, jnp.int32)
    for k in range(slots):
        block = jnp.where(k < live[0], lists[0, k], -whole)
        target = jnp.where(
            lane // SHELL_COL == k, block * SHELL_COL + lane % SHELL_COL, target
        )
    pick_out[...] = jnp.where(iota((whole, cols), 0) == target, 1.0, 0.0).astype(BF16)
    slab_load.wait()


def mix_kernel(n, halves, got, coupling, out):
    pairs = coupling.shape[0]
    sums = []
    for h in range(halves):
        total = got[h].astype(F32)
        for s in range(1, n):
            total = total + got[s * halves + h].astype(F32)
        sums.append(total)
    ao = jnp.concatenate(sums, axis=0).astype(BF16)
    mixed = dot(coupling[...], ao).astype(BF16)
    for d in range(n):
        out[d, :pairs] = mixed
        out[d, pairs:] = jnp.zeros((out.shape[1] - pairs, LANES), BF16)


def raw_kernel(pairs, pick, got, slab, out):
    n, rows, _ = got.shape
    tiles = n // SHELL_ROW
    cols = pick.shape[1]
    slots = cols // SHELL_COL
    held = got[...].reshape(SHELL_ROW, tiles, rows, LANES)
    ao = jnp.concatenate(
        [held[:, t].reshape(SHELL_ROW * rows, LANES) for t in range(tiles)], axis=1
    )
    chosen = dot(ao, pick[...])
    need = -(-pairs // 8) * 8
    per = LANES // SHELL_COL
    group = iota((need, LANES), 1) // SHELL_COL
    turned = {}
    for i in range(SHELL_ROW):
        for t in range(cols // LANES):
            tile = chosen[i * rows : i * rows + need, t * LANES : (t + 1) * LANES]
            for m in range(per):
                turned[i, t, m] = pltpu.roll(tile, m * SHELL_COL, 1) if m else tile
    laid = []
    for k in range(slots):
        t, at = k // per, k % per
        piece = turned[0, t, (0 - at) % per]
        for i in range(1, SHELL_ROW):
            piece = jnp.where(group == i, turned[i, t, (i - at) % per], piece)
        laid.append(piece)
    raw = dot_t(jnp.concatenate(laid, axis=1).astype(BF16), slab[...])
    done = raw[:pairs].astype(BF16)
    for d in range(n):
        out[d] = done


def residual_kernel(nblk, ext_rows, raws, left, right, energies, amp, out, mixed, own_e):
    pairs = raws.shape[1]
    next_ = right.shape[1]

    @pl.when(pl.program_id(0) == 0)
    def _():
        first = lax.axis_index("sp") * ext_rows
        lane_base = pl.multiple_of(first // LANES * LANES, LANES)
        near = energies[:, pl.ds(lane_base, LANES)]
        pick = iota((ext_rows, LANES), 1) == iota((ext_rows, LANES), 0) + (first - lane_base)
        own_e[...] = jnp.sum(jnp.where(pick, near, 0.0), axis=1, keepdims=True)
        for b in range(nblk):
            mixed[:, b, :] = raws[b].astype(F32)

    chunk = amp.shape[0]
    span = SUB * SHELL_COL
    high = SUB * SHELL_ROW
    mask = iota((SUB, SHELL_ROW, WIDTH), 1) == iota((SUB, SHELL_ROW, WIDTH), 2) // SHELL_COL
    tile = jnp.where(
        iota((WIDTH, span), 0) % SHELL_COL == iota((WIDTH, span), 1) % SHELL_COL, 1.0, 0.0
    ).astype(BF16)
    diagonal = iota((high, span), 0) // SHELL_ROW == iota((high, span), 1) // SHELL_COL
    base = pl.program_id(0) * chunk
    uppers = []
    for q in range(chunk):
        columns = []
        for g in range(nblk // SUB):
            block = mixed[base + q, g * SUB : (g + 1) * SUB, :]
            flat = jnp.where(mask, block[:, None, :], 0.0).reshape(high, WIDTH).astype(BF16)
            square = jnp.where(diagonal, dot(flat, tile), 0.0).astype(BF16)
            part = left[g * high : (g + 1) * high, :]
            columns.append(
                lax.dot_general(part, square, (((0,), (0,)), ((), ())), preferred_element_type=F32)
            )
        uppers.append(jnp.concatenate(columns, axis=1).astype(BF16))
    upper = jnp.concatenate(uppers, axis=0)
    inner = dot(upper, right[...]).reshape(chunk, ext_rows, next_)
    diag = own_e[...] + energies[...]
    out[...] = (inner + diag[None] * amp[...].astype(F32)).astype(BF16)


def shards(amplitudes, virtuals, energies, integrals, screened, counts, offsets, coupling):
    pairs, ext_rows, next_ = amplitudes.shape
    nblk = offsets.shape[1]
    n = lax.axis_size("sp")
    halves = lax.axis_size("pb")
    slots = screened.shape[1]
    span = nblk * SHELL_COL
    chunk = chunk_of(pairs)
    padded = -(-pairs // PACK) * PACK
    plain = pltpu.CompilerParams(vmem_limit_bytes=min(60, nblk) * 1024 * 1024)
    in_hbm = functools.partial(
        pltpu.with_memory_space_constraint, memory_space=pltpu.HBM
    )

    partial, right, left, held, slab, pick = pl.pallas_call(
        functools.partial(back_kernel, nblk, chunk),
        in_specs=[HBM, HBM, pl.BlockSpec(memory_space=pltpu.SMEM), HBM, HBM, HBM],
        out_specs=[VMEM] * 6,
        out_shape=[
            jax.ShapeDtypeStruct((n, halves, pairs, LANES), BF16),
            jax.ShapeDtypeStruct((span, next_), BF16),
            jax.ShapeDtypeStruct((nblk * SHELL_ROW, ext_rows), BF16),
            jax.ShapeDtypeStruct(amplitudes.shape, BF16),
            jax.ShapeDtypeStruct(integrals.shape, BF16),
            jax.ShapeDtypeStruct((span, slots * SHELL_COL), BF16),
        ],
        scratch_shapes=[
            pltpu.SMEM(offsets.shape, jnp.int32),
            pltpu.SMEM(screened.shape, jnp.int32),
            pltpu.VMEM((nblk, RIGHT_WIN, next_), BF16),
            pltpu.VMEM((nblk, LEFT_WIN, LANES), BF16),
            pltpu.VMEM((SHELL_ROW, pairs, span), F32),
            pltpu.SemaphoreType.DMA((2, nblk)),
            pltpu.SemaphoreType.DMA((pairs // chunk + 4,)),
        ],
        compiler_params=plain,
        name="back",
    )(in_hbm(offsets), in_hbm(screened), counts, in_hbm(amplitudes), in_hbm(virtuals), in_hbm(integrals))

    got = lax.all_to_all(
        partial.reshape(n * halves, pairs, LANES), ("sp", "pb"), 0, 0, tiled=True
    )
    ao = pl.pallas_call(
        functools.partial(mix_kernel, n, halves),
        in_specs=[VMEM, VMEM],
        out_specs=VMEM,
        out_shape=jax.ShapeDtypeStruct((n, padded, LANES), BF16),
        compiler_params=plain,
        name="mix",
    )(got, coupling)

    ao_all = lax.all_to_all(ao, "sp", 0, 0, tiled=True)
    raw = pl.pallas_call(
        functools.partial(raw_kernel, pairs),
        in_specs=[VMEM] * 3,
        out_specs=VMEM,
        out_shape=jax.ShapeDtypeStruct((n, pairs, WIDTH), BF16),
        compiler_params=plain,
        name="raw",
    )(pick, ao_all, slab)

    raws = lax.all_to_all(raw, "sp", 0, 0, tiled=True)
    return pl.pallas_call(
        functools.partial(residual_kernel, nblk, ext_rows),
        grid=(pairs // chunk,),
        in_specs=[
            pl.BlockSpec(raws.shape, lambda c: (0, 0, 0)),
            pl.BlockSpec(left.shape, lambda c: (0, 0)),
            pl.BlockSpec(right.shape, lambda c: (0, 0)),
            pl.BlockSpec((1, next_), lambda c: (0, 0)),
            pl.BlockSpec((chunk, ext_rows, next_), lambda c: (c, 0, 0)),
        ],
        out_specs=pl.BlockSpec((chunk, ext_rows, next_), lambda c: (c, 0, 0)),
        out_shape=jax.ShapeDtypeStruct(amplitudes.shape, BF16),
        scratch_shapes=[
            pltpu.VMEM((pairs, nblk, WIDTH), F32),
            pltpu.VMEM((ext_rows, 1), F32),
        ],
        compiler_params=pltpu.CompilerParams(
            dimension_semantics=("arbitrary",),
            vmem_limit_bytes=min(60, nblk) * 1024 * 1024,
        ),
        name="residual",
    )(raws, left, right, energies[None], held)


def solution(mesh):
    return jax.shard_map(
        shards,
        mesh=mesh,
        in_specs=(
            P("pb", "sp", None),
            P(),
            P(),
            P("sp", None),
            P("sp", None),
            P("sp"),
            P(),
            P("pb", None),
        ),
        out_specs=P("pb", "sp", None),
        check_vma=False,
    )
```

```python
import functools

import jax
import jax.numpy as jnp
from jax import lax
from jax.experimental import pallas as pl
from jax.experimental.pallas import tpu as pltpu
from jax.sharding import PartitionSpec as P

SHELL_ROW = 8
SHELL_COL = 16
WIDTH = SHELL_ROW * SHELL_COL
SUB = 16
RIGHT_WIN = 32
LEFT_WIN = 16
LANES = 128
PACK = 32
F32 = jnp.float32
BF16 = jnp.bfloat16
VMEM = pl.BlockSpec(memory_space=pltpu.VMEM)
SMEM = pl.BlockSpec(memory_space=pltpu.SMEM)
HBM = pl.BlockSpec(memory_space=pltpu.HBM)


def iota(shape, dim):
    return lax.broadcasted_iota(jnp.int32, shape, dim)


def dot(a, b):
    return jnp.dot(a, b, preferred_element_type=F32)


def dot_t(a, b):
    return lax.dot_general(a, b, (((1,), (1,)), ((), ())), preferred_element_type=F32)


def chunk_of(pairs):
    return max(c for c in range(1, 6) if pairs % c == 0)


def window(low, size, nao):
    base = jnp.minimum(low // 8 * 8, nao - size)
    return pl.multiple_of(base, 8)


def picks(offs, which, first, count, shell, size, nao):
    cols = count * size
    row, col = iota((shell, cols), 0), iota((shell, cols), 1)
    parts = []
    for t in range(count):
        low = offs[which, first + t]
        delta = low - window(low, size, nao) + t * size
        parts.append(jnp.where(col == row + delta, 1.0, 0.0))
    return jnp.concatenate(parts, axis=0).astype(BF16)


def back_kernel(
    nblk, offs_in, lists_in, live, amp, virt, slab,
    out, right, left_wide, amps, slab_out, pick_out,
    offs, lists, right_win, left_win, left, acc, sems, amp_sems,
):
    pairs, ext_rows, next_ = amp.shape
    nao = virt.shape[0]
    slots = lists.shape[1]
    whole, cols = nblk * SHELL_COL, slots * SHELL_COL
    first = lax.axis_index("sp") * ext_rows
    lane_base = pl.multiple_of(first // LANES * LANES, LANES)
    shift = first - lane_base
    facts = [
        pltpu.make_async_copy(offs_in, offs, amp_sems.at[0]),
        pltpu.make_async_copy(lists_in, lists, amp_sems.at[1]),
    ]
    for fact in facts:
        fact.start()
    amp_load = pltpu.make_async_copy(amp, amps, amp_sems.at[2])
    amp_load.start()
    facts[0].wait()
    rights, lefts = [], []
    for b in range(nblk):
        base = window(offs[1, b], RIGHT_WIN, nao)
        rights.append(
            pltpu.make_async_copy(
                virt.at[pl.ds(base, RIGHT_WIN), :], right_win.at[b], sems.at[0, b]
            )
        )
        rights[-1].start()
    for b in range(nblk):
        base = window(offs[0, b], LEFT_WIN, nao)
        lefts.append(
            pltpu.make_async_copy(
                virt.at[pl.ds(base, LEFT_WIN), pl.ds(lane_base, LANES)],
                left_win.at[b],
                sems.at[1, b],
            )
        )
        lefts[-1].start()
    slab_load = pltpu.make_async_copy(slab, slab_out, amp_sems.at[3])
    slab_load.start()

    half_sub = SUB // 2
    right_picks = [
        picks(offs, 1, g * half_sub, half_sub, SHELL_COL, RIGHT_WIN, nao)
        for g in range(nblk // half_sub)
    ]
    left_picks = [
        picks(offs, 0, g * SUB, SUB, SHELL_ROW, LEFT_WIN, nao) for g in range(nblk // SUB)
    ]
    lane_pick = jnp.where(
        iota((LANES, ext_rows), 0) == iota((LANES, ext_rows), 1) + shift, 1.0, 0.0
    ).astype(BF16)
    high, span = SUB * SHELL_ROW, SUB * SHELL_COL
    facts[1].wait()
    lane = iota((1, cols), 1)
    target = jnp.full((1, cols), -1, jnp.int32)
    for k in range(slots):
        block = jnp.where(k < live[0], lists[0, k], -whole)
        target = jnp.where(
            lane // SHELL_COL == k, block * SHELL_COL + lane % SHELL_COL, target
        )
    pick_out[...] = jnp.where(iota((whole, cols), 0) == target, 1.0, 0.0).astype(BF16)

    for load in rights:
        load.wait()
    rows, depth = half_sub * SHELL_COL, half_sub * RIGHT_WIN
    for g, pick in enumerate(right_picks):
        win = right_win[g * half_sub : (g + 1) * half_sub].reshape(depth, next_)
        right[g * rows : (g + 1) * rows, :] = dot(pick, win).astype(BF16)
    for load in lefts:
        load.wait()
    for g, pick in enumerate(left_picks):
        win = left_win[g * SUB : (g + 1) * SUB].reshape(SUB * LEFT_WIN, LANES)
        wide = dot(pick, win).astype(BF16)
        part = dot(wide, lane_pick).astype(BF16)
        left[g * high : (g + 1) * high, :] = part
        down, across = iota((high, span), 0), iota((high, span), 1)
        for i in range(SHELL_ROW):
            place = (down // SHELL_ROW == across // SHELL_COL) & (down % SHELL_ROW == i)
            left_wide[i, :, g * span : (g + 1) * span] = lax.dot_general(
                part,
                jnp.where(place, 1.0, 0.0).astype(BF16),
                (((0,), (0,)), ((), ())),
                preferred_element_type=F32,
            )

    block_of = iota((SHELL_ROW, span), 1) // SHELL_COL
    amp_load.wait()
    half = dot_t(amps[...].reshape(pairs * ext_rows, next_), right[...]).astype(BF16)
    for q in range(pairs):
        own = half[q * ext_rows : (q + 1) * ext_rows]
        for g in range(nblk // SUB):
            full = dot(left[g * high : (g + 1) * high, :], own[:, g * span : (g + 1) * span])
            kept = full[:SHELL_ROW]
            for t in range(1, SUB):
                kept = jnp.where(
                    block_of == t, full[t * SHELL_ROW : (t + 1) * SHELL_ROW], kept
                )
            acc[:, q, g * span : (g + 1) * span] = kept
    tiles = whole // LANES
    for i in range(SHELL_ROW):
        for t in range(tiles):
            done = acc[i, :, t * LANES : (t + 1) * LANES].astype(BF16)
            for h in range(out.shape[1]):
                out[i * tiles + t, h] = done
    slab_load.wait()


def mix_kernel(n, halves, got, coupling, out):
    pairs = coupling.shape[0]
    sums = []
    for h in range(halves):
        total = got[h].astype(F32)
        for s in range(1, n):
            total = total + got[s * halves + h].astype(F32)
        sums.append(total)
    ao = jnp.concatenate(sums, axis=0).astype(BF16)
    mixed = dot(coupling[...], ao).astype(BF16)
    for d in range(n):
        out[d, :pairs] = mixed
        out[d, pairs:] = jnp.zeros((out.shape[1] - pairs, LANES), BF16)


def raw_kernel(pairs, pick, got, slab, out):
    n, rows, _ = got.shape
    tiles = n // SHELL_ROW
    cols = pick.shape[1]
    slots = cols // SHELL_COL
    held = got[...].reshape(SHELL_ROW, tiles, rows, LANES)
    ao = jnp.concatenate(
        [held[:, t].reshape(SHELL_ROW * rows, LANES) for t in range(tiles)], axis=1
    )
    chosen = dot(ao, pick[...])
    need = -(-pairs // 8) * 8
    per = LANES // SHELL_COL
    group = iota((need, LANES), 1) // SHELL_COL
    turned = {}
    for i in range(SHELL_ROW):
        for t in range(cols // LANES):
            tile = chosen[i * rows : i * rows + need, t * LANES : (t + 1) * LANES]
            for m in range(per):
                turned[i, t, m] = pltpu.roll(tile, m * SHELL_COL, 1) if m else tile
    laid = []
    for k in range(slots):
        t, at = k // per, k % per
        piece = turned[0, t, (0 - at) % per]
        for i in range(1, SHELL_ROW):
            piece = jnp.where(group == i, turned[i, t, (i - at) % per], piece)
        laid.append(piece)
    raw = dot_t(jnp.concatenate(laid, axis=1).astype(BF16), slab[...])
    done = raw[:pairs].astype(BF16)
    for d in range(n):
        out[d] = done


def residual_kernel(nblk, chunk, raws, left_wide, right, energies, amp, out, mixed, result, sems):
    n, pairs, _ = raws.shape
    ext_rows, next_ = amp.shape[1:]
    first = lax.axis_index("sp") * ext_rows
    lane_base = pl.multiple_of(first // LANES * LANES, LANES)
    near = energies[:, pl.ds(lane_base, LANES)]
    pick = iota((ext_rows, LANES), 1) == iota((ext_rows, LANES), 0) + (first - lane_base)
    own_e = jnp.sum(jnp.where(pick, near, 0.0), axis=1, keepdims=True)
    per = LANES // SHELL_COL
    group = iota((pairs, LANES), 1) // SHELL_COL
    for t in range(nblk // per):
        tiles = [raws[t * per + m].astype(F32) for m in range(per)]
        turned = {}
        for m in range(per):
            for turn in range(per):
                turned[m, turn] = pltpu.roll(tiles[m], turn * SHELL_COL, 1) if turn else tiles[m]
        for i in range(SHELL_ROW):
            piece = turned[0, (0 - i) % per]
            for m in range(1, per):
                piece = jnp.where(group == m, turned[m, (m - i) % per], piece)
            mixed[i, :, t * LANES : (t + 1) * LANES] = piece

    diag = own_e + energies[...]
    copies = []
    for c in range(pairs // chunk):
        uppers = []
        for q in range(c * chunk, (c + 1) * chunk):
            upper = left_wide[0] * mixed[0, q : q + 1, :]
            for i in range(1, SHELL_ROW):
                upper = upper + left_wide[i] * mixed[i, q : q + 1, :]
            uppers.append(upper.astype(BF16))
        part = pl.ds(c * chunk, chunk)
        inner = dot(jnp.concatenate(uppers, axis=0), right[...]).reshape(chunk, ext_rows, next_)
        result[part] = (inner + diag[None] * amp[part].astype(F32)).astype(BF16)
        copies.append(pltpu.make_async_copy(result.at[part], out.at[part], sems.at[c]))
        copies[-1].start()
    for copy in copies:
        copy.wait()


def shards(amplitudes, virtuals, energies, integrals, screened, counts, offsets, coupling):
    pairs, ext_rows, next_ = amplitudes.shape
    nblk = offsets.shape[1]
    n = lax.axis_size("sp")
    halves = lax.axis_size("pb")
    slots = screened.shape[1]
    span = nblk * SHELL_COL
    chunk = chunk_of(pairs)
    padded = -(-pairs // PACK) * PACK
    plain = pltpu.CompilerParams(vmem_limit_bytes=min(60, nblk) * 1024 * 1024)
    in_hbm = functools.partial(
        pltpu.with_memory_space_constraint, memory_space=pltpu.HBM
    )

    partial, right, left_wide, held, slab, pick = pl.pallas_call(
        functools.partial(back_kernel, nblk),
        in_specs=[HBM, HBM, SMEM, HBM, HBM, HBM],
        out_specs=[VMEM] * 6,
        out_shape=[
            jax.ShapeDtypeStruct((n, halves, pairs, LANES), BF16),
            jax.ShapeDtypeStruct((span, next_), BF16),
            jax.ShapeDtypeStruct((SHELL_ROW, ext_rows, span), F32),
            jax.ShapeDtypeStruct(amplitudes.shape, BF16),
            jax.ShapeDtypeStruct(integrals.shape, BF16),
            jax.ShapeDtypeStruct((span, slots * SHELL_COL), BF16),
        ],
        scratch_shapes=[
            pltpu.SMEM(offsets.shape, jnp.int32),
            pltpu.SMEM(screened.shape, jnp.int32),
            pltpu.VMEM((nblk, RIGHT_WIN, next_), BF16),
            pltpu.VMEM((nblk, LEFT_WIN, LANES), BF16),
            pltpu.VMEM((nblk * SHELL_ROW, ext_rows), BF16),
            pltpu.VMEM((SHELL_ROW, pairs, span), F32),
            pltpu.SemaphoreType.DMA((2, nblk)),
            pltpu.SemaphoreType.DMA((4,)),
        ],
        compiler_params=plain,
        name="back",
    )(
        in_hbm(offsets),
        in_hbm(screened),
        counts,
        in_hbm(amplitudes),
        in_hbm(virtuals),
        in_hbm(integrals),
    )

    got = lax.all_to_all(
        partial.reshape(n * halves, pairs, LANES), ("sp", "pb"), 0, 0, tiled=True
    )
    ao = pl.pallas_call(
        functools.partial(mix_kernel, n, halves),
        in_specs=[VMEM, VMEM],
        out_specs=VMEM,
        out_shape=jax.ShapeDtypeStruct((n, padded, LANES), BF16),
        compiler_params=plain,
        name="mix",
    )(got, coupling)

    ao_all = lax.all_to_all(ao, "sp", 0, 0, tiled=True)
    raw = pl.pallas_call(
        functools.partial(raw_kernel, pairs),
        in_specs=[VMEM] * 3,
        out_specs=VMEM,
        out_shape=jax.ShapeDtypeStruct((n, pairs, WIDTH), BF16),
        compiler_params=plain,
        name="raw",
    )(pick, ao_all, slab)

    raws = lax.all_to_all(raw, "sp", 0, 0, tiled=True)
    return pl.pallas_call(
        functools.partial(residual_kernel, nblk, chunk),
        in_specs=[VMEM] * 5,
        out_specs=HBM,
        out_shape=jax.ShapeDtypeStruct(amplitudes.shape, BF16),
        scratch_shapes=[
            pltpu.VMEM((SHELL_ROW, pairs, span), F32),
            pltpu.VMEM(amplitudes.shape, BF16),
            pltpu.SemaphoreType.DMA((pairs // chunk,)),
        ],
        compiler_params=plain,
        name="residual",
    )(raws, left_wide, right, energies[None], held)


def solution(mesh):
    return jax.shard_map(
        shards,
        mesh=mesh,
        in_specs=(
            P("pb", "sp", None),
            P(),
            P(),
            P("sp", None),
            P("sp", None),
            P("sp"),
            P(),
            P("pb", None),
        ),
        out_specs=P("pb", "sp", None),
        check_vma=False,
    )
```

```python
import functools

import jax
import jax.numpy as jnp
from jax import lax
from jax.experimental import pallas as pl
from jax.experimental.pallas import tpu as pltpu
from jax.sharding import PartitionSpec as P

SHELL_ROW = 8
SHELL_COL = 16
WIDTH = SHELL_ROW * SHELL_COL
SUB = 16
RIGHT_WIN = 32
LEFT_WIN = 16
LANES = 128
F32 = jnp.float32
BF16 = jnp.bfloat16
VMEM = pl.BlockSpec(memory_space=pltpu.VMEM)
HBM = pl.BlockSpec(memory_space=pltpu.HBM)


def iota(shape, dim):
    return lax.broadcasted_iota(jnp.int32, shape, dim)


def dot(a, b):
    return jnp.dot(a, b, preferred_element_type=F32)


def dot_t(a, b):
    return lax.dot_general(a, b, (((1,), (1,)), ((), ())), preferred_element_type=F32)


def chunk_of(pairs):
    return max(c for c in range(1, 6) if pairs % c == 0)


def window(low, size, nao):
    base = jnp.minimum(low // 8 * 8, nao - size)
    return pl.multiple_of(base, 8)


def picks(offs, which, first, count, shell, size, nao):
    cols = count * size
    row, col = iota((shell, cols), 0), iota((shell, cols), 1)
    parts = []
    for t in range(count):
        low = offs[which, first + t]
        delta = low - window(low, size, nao) + t * size
        parts.append(jnp.where(col == row + delta, 1.0, 0.0))
    return jnp.concatenate(parts, axis=0).astype(BF16)


def back_kernel(
    nblk, offs_in, lists_in, amp, virt, slab,
    out, right, left_wide, amps, slab_out, pick_out,
    offs, lists, right_win, left_win, left, sems, amp_sems,
):
    pairs, ext_rows, next_ = amp.shape
    nao = virt.shape[0]
    slots = lists.shape[1]
    whole, cols = nblk * SHELL_COL, slots * SHELL_COL
    first = lax.axis_index("sp") * ext_rows
    lane_base = pl.multiple_of(first // LANES * LANES, LANES)
    shift = first - lane_base
    facts = [
        pltpu.make_async_copy(offs_in, offs, amp_sems.at[0]),
        pltpu.make_async_copy(lists_in, lists, amp_sems.at[1]),
    ]
    for fact in facts:
        fact.start()
    amp_load = pltpu.make_async_copy(amp, amps, amp_sems.at[2])
    amp_load.start()
    facts[0].wait()
    rights, lefts = [], []
    for b in range(nblk):
        base = window(offs[0, b], LEFT_WIN, nao)
        lefts.append(
            pltpu.make_async_copy(
                virt.at[pl.ds(base, LEFT_WIN), pl.ds(lane_base, LANES)],
                left_win.at[b],
                sems.at[1, b],
            )
        )
        lefts[-1].start()
    for b in range(nblk):
        base = window(offs[1, b], RIGHT_WIN, nao)
        rights.append(
            pltpu.make_async_copy(
                virt.at[pl.ds(base, RIGHT_WIN), :], right_win.at[b], sems.at[0, b]
            )
        )
        rights[-1].start()
    slab_load = pltpu.make_async_copy(slab, slab_out, amp_sems.at[3])
    slab_load.start()

    half_sub = SUB // 2
    right_picks = [
        picks(offs, 1, g * half_sub, half_sub, SHELL_COL, RIGHT_WIN, nao)
        for g in range(nblk // half_sub)
    ]
    left_picks = [
        picks(offs, 0, g * SUB, SUB, SHELL_ROW, LEFT_WIN, nao) for g in range(nblk // SUB)
    ]
    lane_pick = jnp.where(
        iota((LANES, ext_rows), 0) == iota((LANES, ext_rows), 1) + shift, 1.0, 0.0
    ).astype(BF16)
    high, span = SUB * SHELL_ROW, SUB * SHELL_COL
    facts[1].wait()
    lane = iota((1, cols), 1)
    target = jnp.full((1, cols), -1, jnp.int32)
    for k in range(slots):
        place = lists[0, k] * SHELL_COL + lane % SHELL_COL
        target = jnp.where(lane // SHELL_COL == k, place, target)
    pick_out[...] = jnp.where(iota((whole, cols), 0) == target, 1.0, 0.0).astype(BF16)

    for load in lefts:
        load.wait()
    for g, pick in enumerate(left_picks):
        win = left_win[g * SUB : (g + 1) * SUB].reshape(SUB * LEFT_WIN, LANES)
        wide = dot(pick, win).astype(BF16)
        part = dot(wide, lane_pick).astype(BF16)
        left[g * high : (g + 1) * high, :] = part
        down, across = iota((high, span), 0), iota((high, span), 1)
        for i in range(SHELL_ROW):
            place = (down // SHELL_ROW == across // SHELL_COL) & (down % SHELL_ROW == i)
            left_wide[i, :, g * span : (g + 1) * span] = lax.dot_general(
                part,
                jnp.where(place, 1.0, 0.0).astype(BF16),
                (((0,), (0,)), ((), ())),
                preferred_element_type=F32,
            )
    for load in rights:
        load.wait()
    rows, depth = half_sub * SHELL_COL, half_sub * RIGHT_WIN
    for g, pick in enumerate(right_picks):
        win = right_win[g * half_sub : (g + 1) * half_sub].reshape(depth, next_)
        right[g * rows : (g + 1) * rows, :] = dot(pick, win).astype(BF16)

    block_of = iota((SHELL_ROW, span), 1) // SHELL_COL
    amp_load.wait()
    half = dot_t(amps[...].reshape(pairs * ext_rows, next_), right[...]).astype(BF16)
    for q in range(pairs):
        own = half[q * ext_rows : (q + 1) * ext_rows]
        for g in range(nblk // SUB):
            full = dot(left[g * high : (g + 1) * high, :], own[:, g * span : (g + 1) * span])
            kept = full[:SHELL_ROW]
            for t in range(1, SUB):
                kept = jnp.where(
                    block_of == t, full[t * SHELL_ROW : (t + 1) * SHELL_ROW], kept
                )
            rows = slice(q * SHELL_ROW, (q + 1) * SHELL_ROW)
            out[rows, g * span : (g + 1) * span] = kept.astype(BF16)
    slab_load.wait()


def add_up(parts):
    total = parts[0][...].astype(F32)
    for part in parts[1:]:
        total = total + part[...].astype(F32)
    return total.astype(BF16)


def sum_kernel(*refs):
    refs[-1][...] = add_up(refs[:-1])


def raw_kernel(pairs, live, pick, slab, *refs):
    parts, out, chosen = refs[:-2], refs[-2], refs[-1]
    cols = pick.shape[1]
    slots = cols // SHELL_COL
    result = dot(add_up(parts), pick[...])
    for t in range(cols // LANES):
        chosen[t] = result[:, t * LANES : (t + 1) * LANES]
    per = LANES // SHELL_COL
    group = iota((pairs, LANES), 1) // SHELL_COL
    count = live[...]
    turned = {}
    for i in range(SHELL_ROW):
        for t in range(cols // LANES):
            tile = chosen[t, pl.ds(i, pairs, stride=SHELL_ROW), :]
            for m in range(per):
                turned[i, t, m] = pltpu.roll(tile, m * SHELL_COL, 1) if m else tile
    laid = []
    for k in range(slots):
        t, at = k // per, k % per
        piece = turned[0, t, (0 - at) % per]
        for i in range(1, SHELL_ROW):
            piece = jnp.where(group == i, turned[i, t, (i - at) % per], piece)
        laid.append(jnp.where(k < count, piece, 0.0))
    raw = dot_t(jnp.concatenate(laid, axis=1).astype(BF16), slab[...]).astype(BF16)
    for d in range(out.shape[0]):
        out[d] = raw


def residual_kernel(
    nblk, halves, chunk, raws, coupling, left_wide, right, energies, amp, out, mixed, result, sems
):
    pairs = raws.shape[1]
    ext_rows, next_ = amp.shape[1:]
    first = lax.axis_index("sp") * ext_rows
    lane_base = pl.multiple_of(first // LANES * LANES, LANES)
    near = energies[:, pl.ds(lane_base, LANES)]
    pick = iota((ext_rows, LANES), 1) == iota((ext_rows, LANES), 0) + (first - lane_base)
    own_e = jnp.sum(jnp.where(pick, near, 0.0), axis=1, keepdims=True)
    every = jnp.concatenate(
        [
            jnp.concatenate([raws[b * halves + h].astype(F32) for b in range(nblk)], axis=1)
            for h in range(halves)
        ],
        axis=0,
    ).astype(BF16)
    coupled = dot(coupling[...], every).astype(BF16).astype(F32)
    per = LANES // SHELL_COL
    group = iota((pairs, LANES), 1) // SHELL_COL
    for t in range(nblk // per):
        tiles = [
            coupled[:, (t * per + m) * WIDTH : (t * per + m + 1) * WIDTH] for m in range(per)
        ]
        turned = {}
        for m in range(per):
            for turn in range(per):
                turned[m, turn] = pltpu.roll(tiles[m], turn * SHELL_COL, 1) if turn else tiles[m]
        for i in range(SHELL_ROW):
            piece = turned[0, (0 - i) % per]
            for m in range(1, per):
                piece = jnp.where(group == m, turned[m, (m - i) % per], piece)
            mixed[i, :, t * LANES : (t + 1) * LANES] = piece

    diag = own_e + energies[...]
    copies = []
    for c in range(pairs // chunk):
        uppers = []
        for q in range(c * chunk, (c + 1) * chunk):
            upper = left_wide[0] * mixed[0, q : q + 1, :]
            for i in range(1, SHELL_ROW):
                upper = upper + left_wide[i] * mixed[i, q : q + 1, :]
            uppers.append(upper.astype(BF16))
        part = pl.ds(c * chunk, chunk)
        inner = dot(jnp.concatenate(uppers, axis=0), right[...]).reshape(chunk, ext_rows, next_)
        result[part] = (inner + diag[None] * amp[part].astype(F32)).astype(BF16)
        copies.append(pltpu.make_async_copy(result.at[part], out.at[part], sems.at[c]))
        copies[-1].start()
    for copy in copies:
        copy.wait()


def shards(amplitudes, virtuals, energies, integrals, screened, counts, offsets, coupling):
    pairs, ext_rows, next_ = amplitudes.shape
    nblk = offsets.shape[1]
    n = lax.axis_size("sp")
    halves = lax.axis_size("pb")
    slots = screened.shape[1]
    span = nblk * SHELL_COL
    chunk = chunk_of(pairs)
    plain = pltpu.CompilerParams(vmem_limit_bytes=min(60, nblk) * 1024 * 1024)
    in_hbm = functools.partial(
        pltpu.with_memory_space_constraint, memory_space=pltpu.HBM
    )

    partial, right, left_wide, held, slab, pick = pl.pallas_call(
        functools.partial(back_kernel, nblk),
        in_specs=[HBM] * 5,
        out_specs=[VMEM] * 6,
        out_shape=[
            jax.ShapeDtypeStruct((pairs * SHELL_ROW, span), BF16),
            jax.ShapeDtypeStruct((span, next_), BF16),
            jax.ShapeDtypeStruct((SHELL_ROW, ext_rows, span), F32),
            jax.ShapeDtypeStruct(amplitudes.shape, BF16),
            jax.ShapeDtypeStruct(integrals.shape, BF16),
            jax.ShapeDtypeStruct((span, slots * SHELL_COL), BF16),
        ],
        scratch_shapes=[
            pltpu.SMEM(offsets.shape, jnp.int32),
            pltpu.SMEM(screened.shape, jnp.int32),
            pltpu.VMEM((nblk, RIGHT_WIN, next_), BF16),
            pltpu.VMEM((nblk, LEFT_WIN, LANES), BF16),
            pltpu.VMEM((nblk * SHELL_ROW, ext_rows), BF16),
            pltpu.SemaphoreType.DMA((2, nblk)),
            pltpu.SemaphoreType.DMA((4,)),
        ],
        compiler_params=plain,
        name="back",
    )(
        in_hbm(offsets),
        in_hbm(screened),
        in_hbm(amplitudes),
        in_hbm(virtuals),
        in_hbm(integrals),
    )

    def reaches(below, radix):
        def peer(i, turn):
            digit = i // below % radix
            return i + ((digit ^ turn) - digit) * below

        return [
            lax.ppermute(partial, "sp", [(i, peer(i, turn)) for i in range(n)])
            for turn in range(1, radix)
        ]

    stages, below = [], 1
    while below < n:
        stages.append((below, 4 if n // below % 4 == 0 else 2))
        below *= stages[-1][1]
    for below, radix in stages[:-1]:
        parts = [partial] + reaches(below, radix)
        partial = pl.pallas_call(
            sum_kernel,
            in_specs=[VMEM] * len(parts),
            out_specs=VMEM,
            out_shape=jax.ShapeDtypeStruct(partial.shape, BF16),
            compiler_params=plain,
            name="sum",
        )(*parts)
    parts = [partial] + reaches(*stages[-1])
    raw = pl.pallas_call(
        functools.partial(raw_kernel, pairs),
        in_specs=[VMEM] * (3 + len(parts)),
        out_specs=VMEM,
        out_shape=jax.ShapeDtypeStruct((n * halves, pairs, WIDTH), BF16),
        scratch_shapes=[pltpu.VMEM((slots * SHELL_COL // LANES, pairs * SHELL_ROW, LANES), F32)],
        compiler_params=plain,
        name="raw",
    )(counts[None], pick, slab, *parts)

    raws = lax.all_to_all(raw, ("sp", "pb"), 0, 0, tiled=True)
    return pl.pallas_call(
        functools.partial(residual_kernel, nblk, halves, chunk),
        in_specs=[VMEM] * 6,
        out_specs=HBM,
        out_shape=jax.ShapeDtypeStruct(amplitudes.shape, BF16),
        scratch_shapes=[
            pltpu.VMEM((SHELL_ROW, pairs, span), F32),
            pltpu.VMEM(amplitudes.shape, BF16),
            pltpu.SemaphoreType.DMA((pairs // chunk,)),
        ],
        compiler_params=plain,
        name="residual",
    )(raws, coupling, left_wide, right, energies[None], held)


def solution(mesh):
    return jax.shard_map(
        shards,
        mesh=mesh,
        in_specs=(
            P("pb", "sp", None),
            P(),
            P(),
            P("sp", None),
            P("sp", None),
            P("sp"),
            P(),
            P("pb", None),
        ),
        out_specs=P("pb", "sp", None),
        check_vma=False,
    )
```

```python
import functools

import jax
import jax.numpy as jnp
from jax import lax
from jax.experimental import pallas as pl
from jax.experimental.pallas import tpu as pltpu
from jax.sharding import PartitionSpec as P

SHELL_ROW = 8
SHELL_COL = 16
WIDTH = SHELL_ROW * SHELL_COL
RIGHT_WIN = 24
LEFT_WIN = 16
LANES = 128
F32 = jnp.float32
BF16 = jnp.bfloat16
VMEM = pl.BlockSpec(memory_space=pltpu.VMEM)
HBM = pl.BlockSpec(memory_space=pltpu.HBM)


def iota(shape, dim):
    return lax.broadcasted_iota(jnp.int32, shape, dim)


def split(index, size):
    return index >> (size.bit_length() - 1), index & (size - 1)


def dot(a, b):
    return jnp.dot(a, b, preferred_element_type=F32)


def dot_t(a, b):
    return lax.dot_general(a, b, (((1,), (1,)), ((), ())), preferred_element_type=F32)


def chunk_of(pairs):
    return max(c for c in (1, 5) if pairs % c == 0)


def window(low, size, nao):
    base = jnp.minimum(low & -8, nao - size)
    return pl.multiple_of(base, 8)


def picks(offs, which, first, count, shell, size, nao):
    cols = count * size
    row, col = iota((shell, cols), 0), iota((shell, cols), 1)
    parts = []
    for t in range(count):
        low = offs[which, first + t]
        delta = low - window(low, size, nao) + t * size
        parts.append(jnp.where(col == row + delta, 1.0, 0.0))
    return jnp.concatenate(parts, axis=0).astype(BF16)


def back_kernel(
    nblk, offs_in, amp, virt, out, right, left, amps,
    offs, right_win, left_win, sems, amp_sems,
):
    pairs, ext_rows, next_ = amp.shape
    nao = virt.shape[0]
    whole = nblk * SHELL_COL
    first = lax.axis_index("sp") * ext_rows
    lane_base = pl.multiple_of(first & -LANES, LANES)
    shift = first - lane_base
    offs_load = pltpu.make_async_copy(offs_in, offs, amp_sems.at[0])
    offs_load.start()
    amp_load = pltpu.make_async_copy(amp, amps, amp_sems.at[1])
    amp_load.start()
    offs_load.wait()
    rights, lefts = [], []
    for b in range(nblk):
        base = window(offs[0, b], LEFT_WIN, nao)
        lefts.append(
            pltpu.make_async_copy(
                virt.at[pl.ds(base, LEFT_WIN), pl.ds(lane_base, LANES)],
                left_win.at[b],
                sems.at[1, b],
            )
        )
        lefts[-1].start()
    for b in range(nblk):
        base = window(offs[1, b], RIGHT_WIN, nao)
        rights.append(
            pltpu.make_async_copy(
                virt.at[pl.ds(base, RIGHT_WIN), :], right_win.at[b], sems.at[0, b]
            )
        )
        rights[-1].start()

    per = LANES // SHELL_COL
    right_picks = [
        picks(offs, 1, t * per, per, SHELL_COL, RIGHT_WIN, nao)
        for t in range(whole // LANES)
    ]
    left_picks = [
        picks(offs, 0, t * per, per, SHELL_ROW, LEFT_WIN, nao) for t in range(whole // LANES)
    ]
    lane_pick = jnp.where(
        iota((ext_rows, LANES), 1) == iota((ext_rows, LANES), 0) + shift, 1.0, 0.0
    ).astype(BF16)
    for load in lefts:
        load.wait()
    left_rows = []
    for t, pick in enumerate(left_picks):
        win = left_win[t * per : (t + 1) * per].reshape(per * LEFT_WIN, LANES)
        wide = dot(pick, win).astype(BF16)
        left[t] = dot_t(lane_pick, wide).astype(BF16)
        left_rows.append(dot_t(wide, lane_pick).astype(BF16))
    for load in rights:
        load.wait()
    for t, pick in enumerate(right_picks):
        win = right_win[t * per : (t + 1) * per].reshape(per * RIGHT_WIN, next_)
        right[t * LANES : (t + 1) * LANES, :] = dot(pick, win).astype(BF16)

    amp_load.wait()
    half = dot_t(amps[...].reshape(pairs * ext_rows, next_), right[...]).astype(BF16)
    side = 2 if pairs % 2 == 0 else 1
    block_of, _ = split(iota((SHELL_ROW, side * LANES), 1) & (LANES - 1), SHELL_COL)
    for q in range(0, pairs, side):
        for t in range(whole // LANES):
            lanes = slice(t * LANES, (t + 1) * LANES)
            beside = jnp.concatenate(
                [half[(q + u) * ext_rows : (q + u + 1) * ext_rows, lanes] for u in range(side)],
                axis=1,
            )
            full = dot(left_rows[t], beside)
            kept = full[:SHELL_ROW]
            for m in range(1, per):
                kept = jnp.where(block_of == m, full[m * SHELL_ROW : (m + 1) * SHELL_ROW], kept)
            for u in range(side):
                rows = slice((q + u) * SHELL_ROW, (q + u + 1) * SHELL_ROW)
                out[rows, lanes] = kept[:, u * LANES : (u + 1) * LANES].astype(BF16)


def ready_kernel(
    nblk, ext_rows, lists_in, slab, energies, amps, product, pick_out, slab_out, lists, sems
):
    load = pltpu.make_async_copy(lists_in, lists, sems.at[0])
    load.start()
    slab_load = pltpu.make_async_copy(slab, slab_out, sems.at[1])
    slab_load.start()
    first = lax.axis_index("sp") * ext_rows
    lane_base = pl.multiple_of(first & -LANES, LANES)
    near = energies[:, pl.ds(lane_base, LANES)]
    own = iota((ext_rows, LANES), 1) == iota((ext_rows, LANES), 0) + (first - lane_base)
    own_e = jnp.sum(jnp.where(own, near, 0.0), axis=1, keepdims=True)
    diag = own_e + energies[...]
    for q in range(amps.shape[0]):
        product[q] = diag * amps[q].astype(F32)
    slots = lists.shape[1]
    whole, cols = nblk * SHELL_COL, slots * SHELL_COL
    load.wait()
    slot, inner = split(iota((1, cols), 1), SHELL_COL)
    target = jnp.full((1, cols), -1, jnp.int32)
    for k in range(slots):
        target = jnp.where(slot == k, lists[0, k] * SHELL_COL + inner, target)
    pick_out[...] = jnp.where(iota((whole, cols), 0) == target, 1.0, 0.0).astype(BF16)
    slab_load.wait()


def regroup(tiles):
    per = len(tiles)
    group, _ = split(iota(tiles[0].shape, 1), SHELL_COL)
    turned = [
        [pltpu.roll(tile, turn * SHELL_COL, 1) if turn else tile for turn in range(per)]
        for tile in tiles
    ]
    pieces = []
    for m in range(per):
        piece = turned[0][-m % per]
        for i in range(1, per):
            piece = jnp.where(group == i, turned[i][(i - m) % per], piece)
        pieces.append(piece)
    return pieces


def add_up(parts):
    total = parts[0][...].astype(F32)
    for part in parts[1:]:
        total = total + part[...].astype(F32)
    return total.astype(BF16)


def sum_kernel(*refs):
    refs[-1][...] = add_up(refs[:-1])


def raw_kernel(pairs, live, pick, slab, *refs):
    parts, out, chosen = refs[:-2], refs[-2], refs[-1]
    cols = pick.shape[1]
    result = dot(add_up(parts), pick[...])
    for t in range(cols // LANES):
        chosen[t] = result[:, t * LANES : (t + 1) * LANES]
    per = LANES // SHELL_COL
    count = live[...]
    laid = []
    for t in range(cols // LANES):
        tiles = [chosen[t, pl.ds(i, pairs, stride=SHELL_ROW), :] for i in range(SHELL_ROW)]
        for m, piece in enumerate(regroup(tiles)):
            laid.append(jnp.where(t * per + m < count, piece, 0.0))
    raw = dot_t(jnp.concatenate(laid, axis=1).astype(BF16), slab[...]).astype(BF16)
    for d in range(out.shape[0]):
        out[d] = raw


def residual_kernel(
    nblk, halves, chunk, raws, coupling, left, right, product, out, mixed, upper, result, sems
):
    pairs = raws.shape[1]
    ext_rows, next_ = product.shape[1:]
    every = jnp.concatenate(
        [
            jnp.concatenate([raws[b * halves + h].astype(F32) for b in range(nblk)], axis=1)
            for h in range(halves)
        ],
        axis=0,
    ).astype(BF16)
    coupled = dot(coupling[...], every).astype(BF16).astype(F32)
    per = LANES // SHELL_COL
    for t in range(nblk // per):
        tiles = [
            coupled[:, (t * per + m) * WIDTH : (t * per + m + 1) * WIDTH] for m in range(per)
        ]
        for i, piece in enumerate(regroup(tiles)):
            mixed[t, pl.ds(i, pairs, stride=SHELL_ROW), :] = piece

    side = 2 if pairs % 2 == 0 else 1
    block_of, _ = split(iota((SHELL_ROW, side * LANES), 1) & (LANES - 1), SHELL_COL)
    for q in range(0, pairs, side):
        columns = []
        for t in range(nblk // per):
            squares = jnp.concatenate(
                [mixed[t, (q + u) * SHELL_ROW : (q + u + 1) * SHELL_ROW, :] for u in range(side)],
                axis=1,
            )
            stack = [jnp.where(block_of == m, squares, 0.0) for m in range(per)]
            columns.append(dot(left[t], jnp.concatenate(stack, axis=0).astype(BF16)))
        for u in range(side):
            lanes = slice(u * LANES, (u + 1) * LANES)
            upper[q + u] = jnp.concatenate([x[:, lanes] for x in columns], axis=1).astype(BF16)
    copies = []
    for c in range(pairs // chunk):
        part = pl.ds(c * chunk, chunk)
        flat = upper[part].reshape(chunk * ext_rows, nblk * SHELL_COL)
        inner = dot(flat, right[...]).reshape(chunk, ext_rows, next_)
        result[part] = (inner + product[part]).astype(BF16)
        copies.append(pltpu.make_async_copy(result.at[part], out.at[part], sems.at[c]))
        copies[-1].start()
    for copy in copies:
        copy.wait()


def shards(amplitudes, virtuals, energies, integrals, screened, counts, offsets, coupling):
    pairs, ext_rows, next_ = amplitudes.shape
    nblk = offsets.shape[1]
    n = lax.axis_size("sp")
    halves = lax.axis_size("pb")
    slots = screened.shape[1]
    span = nblk * SHELL_COL
    chunk = chunk_of(pairs)
    plain = pltpu.CompilerParams(vmem_limit_bytes=min(60, nblk) * 1024 * 1024)
    in_hbm = functools.partial(
        pltpu.with_memory_space_constraint, memory_space=pltpu.HBM
    )

    partial, right, left, held = pl.pallas_call(
        functools.partial(back_kernel, nblk),
        in_specs=[HBM] * 3,
        out_specs=[VMEM] * 4,
        out_shape=[
            jax.ShapeDtypeStruct((pairs * SHELL_ROW, span), BF16),
            jax.ShapeDtypeStruct((span, next_), BF16),
            jax.ShapeDtypeStruct((span // LANES, ext_rows, LANES // SHELL_COL * SHELL_ROW), BF16),
            jax.ShapeDtypeStruct(amplitudes.shape, BF16),
        ],
        scratch_shapes=[
            pltpu.SMEM(offsets.shape, jnp.int32),
            pltpu.VMEM((nblk, RIGHT_WIN, next_), BF16),
            pltpu.VMEM((nblk, LEFT_WIN, LANES), BF16),
            pltpu.SemaphoreType.DMA((2, nblk)),
            pltpu.SemaphoreType.DMA((3,)),
        ],
        compiler_params=plain,
        name="back",
    )(in_hbm(offsets), in_hbm(amplitudes), in_hbm(virtuals))

    product, pick, slab = pl.pallas_call(
        functools.partial(ready_kernel, nblk, ext_rows),
        in_specs=[HBM, HBM, VMEM, VMEM],
        out_specs=[VMEM] * 3,
        out_shape=[
            jax.ShapeDtypeStruct(amplitudes.shape, F32),
            jax.ShapeDtypeStruct((span, slots * SHELL_COL), BF16),
            jax.ShapeDtypeStruct(integrals.shape, BF16),
        ],
        scratch_shapes=[
            pltpu.SMEM(screened.shape, jnp.int32),
            pltpu.SemaphoreType.DMA((2,)),
        ],
        compiler_params=plain,
        name="ready",
    )(in_hbm(screened), in_hbm(integrals), energies[None], held)

    stages, below = [], 1
    while below < n:
        stages.append((below, 4 if n // below % 4 == 0 else 2))
        below *= stages[-1][1]
    turned = len({radix for _, radix in stages}) == 1

    def peer(step, turn, i, h):
        below, radix = stages[(step + h * turned) % len(stages)]
        digit = i // below % radix
        return i + ((digit ^ turn) - digit) * below

    def reaches(step):
        parts = []
        for turn in range(1, stages[step][1]):
            ring = [
                (i * halves + h, peer(step, turn, i, h) * halves + h)
                for i in range(n)
                for h in range(halves)
            ]
            parts.append(lax.ppermute(partial, ("sp", "pb"), ring))
        return parts

    for step in range(len(stages) - 1):
        parts = [partial] + reaches(step)
        partial = pl.pallas_call(
            sum_kernel,
            in_specs=[VMEM] * len(parts),
            out_specs=VMEM,
            out_shape=jax.ShapeDtypeStruct(partial.shape, BF16),
            compiler_params=plain,
            name="sum",
        )(*parts)
    parts = [partial] + reaches(len(stages) - 1)
    raw = pl.pallas_call(
        functools.partial(raw_kernel, pairs),
        in_specs=[VMEM] * (3 + len(parts)),
        out_specs=VMEM,
        out_shape=jax.ShapeDtypeStruct((n * halves, pairs, WIDTH), BF16),
        scratch_shapes=[pltpu.VMEM((slots * SHELL_COL // LANES, pairs * SHELL_ROW, LANES), F32)],
        compiler_params=plain,
        name="raw",
    )(counts[None], pick, slab, *parts)

    raws = lax.all_to_all(raw, ("sp", "pb"), 0, 0, tiled=True)
    return pl.pallas_call(
        functools.partial(residual_kernel, nblk, halves, chunk),
        in_specs=[VMEM] * 5,
        out_specs=HBM,
        out_shape=jax.ShapeDtypeStruct(amplitudes.shape, BF16),
        scratch_shapes=[
            pltpu.VMEM((span // LANES, pairs * SHELL_ROW, LANES), F32),
            pltpu.VMEM((pairs, ext_rows, span), BF16),
            pltpu.VMEM(amplitudes.shape, BF16),
            pltpu.SemaphoreType.DMA((pairs // chunk,)),
        ],
        compiler_params=plain,
        name="residual",
    )(raws, coupling, left, right, product)


def solution(mesh):
    return jax.shard_map(
        shards,
        mesh=mesh,
        in_specs=(
            P("pb", "sp", None),
            P(),
            P(),
            P("sp", None),
            P("sp", None),
            P("sp"),
            P(),
            P("pb", None),
        ),
        out_specs=P("pb", "sp", None),
        check_vma=False,
    )
```

```python
import functools

import jax
import jax.numpy as jnp
from jax import lax
from jax.experimental import pallas as pl
from jax.experimental.pallas import tpu as pltpu
from jax.sharding import PartitionSpec as P

SHELL_ROW = 8
SHELL_COL = 16
WIDTH = SHELL_ROW * SHELL_COL
RIGHT_WIN = 24
LEFT_WIN = 16
LANES = 128
F32 = jnp.float32
BF16 = jnp.bfloat16
VMEM = pl.BlockSpec(memory_space=pltpu.VMEM)
HBM = pl.BlockSpec(memory_space=pltpu.HBM)


def iota(shape, dim):
    return lax.broadcasted_iota(jnp.int32, shape, dim)


def split(index, size):
    return index >> (size.bit_length() - 1), index & (size - 1)


def dot(a, b):
    return jnp.dot(a, b, preferred_element_type=F32)


def dot_t(a, b):
    return lax.dot_general(a, b, (((1,), (1,)), ((), ())), preferred_element_type=F32)


def chunk_of(pairs):
    return max(c for c in (1, 5) if pairs % c == 0)


def window(low, size, nao):
    base = jnp.minimum(low & -8, nao - size)
    return pl.multiple_of(base, 8)


def picks(offs, which, first, count, shell, size, nao):
    cols = count * size
    row, col = iota((shell, cols), 0), iota((shell, cols), 1)
    parts = []
    for t in range(count):
        low = offs[which, first + t]
        delta = low - window(low, size, nao) + t * size
        parts.append(jnp.where(col == row + delta, 1.0, 0.0))
    return jnp.concatenate(parts, axis=0).astype(BF16)


def back_kernel(
    nblk, offs_in, amp, virt, out, right, left, amps,
    offs, right_win, left_win, sems, amp_sems,
):
    pairs, ext_rows, next_ = amp.shape
    nao = virt.shape[0]
    whole = nblk * SHELL_COL
    first = lax.axis_index("sp") * ext_rows
    lane_base = pl.multiple_of(first & -LANES, LANES)
    shift = first - lane_base
    offs_load = pltpu.make_async_copy(offs_in, offs, amp_sems.at[0])
    offs_load.start()
    amp_load = pltpu.make_async_copy(amp, amps, amp_sems.at[1])
    amp_load.start()
    offs_load.wait()
    rights, lefts = [], []
    for b in range(nblk):
        base = window(offs[0, b], LEFT_WIN, nao)
        lefts.append(
            pltpu.make_async_copy(
                virt.at[pl.ds(base, LEFT_WIN), pl.ds(lane_base, LANES)],
                left_win.at[b],
                sems.at[1, b],
            )
        )
        lefts[-1].start()
    for b in range(nblk):
        base = window(offs[1, b], RIGHT_WIN, nao)
        rights.append(
            pltpu.make_async_copy(
                virt.at[pl.ds(base, RIGHT_WIN), :], right_win.at[b], sems.at[0, b]
            )
        )
        rights[-1].start()

    per = LANES // SHELL_COL
    right_picks = [
        picks(offs, 1, t * per, per, SHELL_COL, RIGHT_WIN, nao)
        for t in range(whole // LANES)
    ]
    left_picks = [
        picks(offs, 0, t * per, per, SHELL_ROW, LEFT_WIN, nao) for t in range(whole // LANES)
    ]
    lane_pick = jnp.where(
        iota((ext_rows, LANES), 1) == iota((ext_rows, LANES), 0) + shift, 1.0, 0.0
    ).astype(BF16)
    for load in lefts:
        load.wait()
    left_rows = []
    for t, pick in enumerate(left_picks):
        win = left_win[t * per : (t + 1) * per].reshape(per * LEFT_WIN, LANES)
        wide = dot(pick, win).astype(BF16)
        left[t] = dot_t(lane_pick, wide).astype(BF16)
        left_rows.append(dot_t(wide, lane_pick).astype(BF16))
    for load in rights:
        load.wait()
    for t, pick in enumerate(right_picks):
        win = right_win[t * per : (t + 1) * per].reshape(per * RIGHT_WIN, next_)
        right[t * LANES : (t + 1) * LANES, :] = dot(pick, win).astype(BF16)

    amp_load.wait()
    half = dot_t(amps[...].reshape(pairs * ext_rows, next_), right[...]).astype(BF16)
    side = 2 if pairs % 2 == 0 else 1
    block_of, _ = split(iota((SHELL_ROW, side * LANES), 1) & (LANES - 1), SHELL_COL)
    for q in range(0, pairs, side):
        for t in range(whole // LANES):
            lanes = slice(t * LANES, (t + 1) * LANES)
            beside = jnp.concatenate(
                [half[(q + u) * ext_rows : (q + u + 1) * ext_rows, lanes] for u in range(side)],
                axis=1,
            )
            full = dot(left_rows[t], beside)
            kept = full[:SHELL_ROW]
            for m in range(1, per):
                kept = jnp.where(block_of == m, full[m * SHELL_ROW : (m + 1) * SHELL_ROW], kept)
            for u in range(side):
                rows = slice((q + u) * SHELL_ROW, (q + u + 1) * SHELL_ROW)
                out[rows, lanes] = kept[:, u * LANES : (u + 1) * LANES].astype(BF16)


def ready_kernel(
    nblk, ext_rows, lists_in, live, slab, energies, amps, product, slab_out, lists, slab_in, sems
):
    load = pltpu.make_async_copy(lists_in, lists, sems.at[0])
    load.start()
    slab_load = pltpu.make_async_copy(slab, slab_in, sems.at[1])
    slab_load.start()
    first = lax.axis_index("sp") * ext_rows
    lane_base = pl.multiple_of(first & -LANES, LANES)
    near = energies[:, pl.ds(lane_base, LANES)]
    own = iota((ext_rows, LANES), 1) == iota((ext_rows, LANES), 0) + (first - lane_base)
    own_e = jnp.sum(jnp.where(own, near, 0.0), axis=1, keepdims=True)
    diag = own_e + energies[...]
    for q in range(amps.shape[0]):
        product[q] = diag * amps[q].astype(F32)
    slots = lists.shape[1]
    if slots < nblk:
        slab_out[...] = jnp.zeros(slab_out.shape, BF16)
    count = live[...]
    load.wait()
    slab_load.wait()
    for k in range(slots):
        to = pl.ds(pl.multiple_of(lists[0, k] * WIDTH, WIDTH), WIDTH)
        kept = jnp.where(k < count, slab_in[:, k * WIDTH : (k + 1) * WIDTH].astype(F32), 0.0)
        slab_out[:, to] = kept.astype(BF16)


def regroup(tiles):
    per = len(tiles)
    group, _ = split(iota(tiles[0].shape, 1), SHELL_COL)
    turned = [
        [pltpu.roll(tile, turn * SHELL_COL, 1) if turn else tile for turn in range(per)]
        for tile in tiles
    ]
    pieces = []
    for m in range(per):
        piece = turned[0][-m % per]
        for i in range(1, per):
            piece = jnp.where(group == i, turned[i][(i - m) % per], piece)
        pieces.append(piece)
    return pieces


def add_up(parts):
    total = parts[0][...].astype(F32)
    for part in parts[1:]:
        total = total + part[...].astype(F32)
    return total


def sum_kernel(*refs):
    refs[-1][...] = add_up(refs[:-1]).astype(BF16)


def raw_kernel(pairs, slab, *refs):
    parts, out, ao = refs[:-2], refs[-2], refs[-1]
    total = add_up(parts)
    laid = []
    for t in range(ao.shape[0]):
        ao[t] = total[:, t * LANES : (t + 1) * LANES]
        laid += regroup([ao[t, pl.ds(i, pairs, stride=SHELL_ROW), :] for i in range(SHELL_ROW)])
    raw = dot_t(jnp.concatenate(laid, axis=1).astype(BF16), slab[...]).astype(BF16)
    for d in range(out.shape[0]):
        out[d] = raw


def residual_kernel(
    nblk, halves, chunk, raws, coupling, left, right, product, out, mixed, upper, result, sems
):
    pairs = raws.shape[1]
    ext_rows, next_ = product.shape[1:]
    every = jnp.concatenate(
        [
            jnp.concatenate([raws[b * halves + h].astype(F32) for b in range(nblk)], axis=1)
            for h in range(halves)
        ],
        axis=0,
    ).astype(BF16)
    coupled = dot(coupling[...], every).astype(BF16).astype(F32)
    per = LANES // SHELL_COL
    for t in range(nblk // per):
        tiles = [
            coupled[:, (t * per + m) * WIDTH : (t * per + m + 1) * WIDTH] for m in range(per)
        ]
        for i, piece in enumerate(regroup(tiles)):
            mixed[t, pl.ds(i, pairs, stride=SHELL_ROW), :] = piece

    side = 2 if pairs % 2 == 0 else 1
    block_of, _ = split(iota((SHELL_ROW, side * LANES), 1) & (LANES - 1), SHELL_COL)
    for q in range(0, pairs, side):
        columns = []
        for t in range(nblk // per):
            squares = jnp.concatenate(
                [mixed[t, (q + u) * SHELL_ROW : (q + u + 1) * SHELL_ROW, :] for u in range(side)],
                axis=1,
            )
            stack = [jnp.where(block_of == m, squares, 0.0) for m in range(per)]
            columns.append(dot(left[t], jnp.concatenate(stack, axis=0).astype(BF16)))
        for u in range(side):
            lanes = slice(u * LANES, (u + 1) * LANES)
            upper[q + u] = jnp.concatenate([x[:, lanes] for x in columns], axis=1).astype(BF16)
    copies = []
    for c in range(pairs // chunk):
        part = pl.ds(c * chunk, chunk)
        flat = upper[part].reshape(chunk * ext_rows, nblk * SHELL_COL)
        inner = dot(flat, right[...]).reshape(chunk, ext_rows, next_)
        result[part] = (inner + product[part]).astype(BF16)
        copies.append(pltpu.make_async_copy(result.at[part], out.at[part], sems.at[c]))
        copies[-1].start()
    for copy in copies:
        copy.wait()


def shards(amplitudes, virtuals, energies, integrals, screened, counts, offsets, coupling):
    pairs, ext_rows, next_ = amplitudes.shape
    nblk = offsets.shape[1]
    n = lax.axis_size("sp")
    halves = lax.axis_size("pb")
    span = nblk * SHELL_COL
    chunk = chunk_of(pairs)
    plain = pltpu.CompilerParams(vmem_limit_bytes=min(60, nblk) * 1024 * 1024)
    in_hbm = functools.partial(
        pltpu.with_memory_space_constraint, memory_space=pltpu.HBM
    )

    partial, right, left, held = pl.pallas_call(
        functools.partial(back_kernel, nblk),
        in_specs=[HBM] * 3,
        out_specs=[VMEM] * 4,
        out_shape=[
            jax.ShapeDtypeStruct((pairs * SHELL_ROW, span), BF16),
            jax.ShapeDtypeStruct((span, next_), BF16),
            jax.ShapeDtypeStruct((span // LANES, ext_rows, LANES // SHELL_COL * SHELL_ROW), BF16),
            jax.ShapeDtypeStruct(amplitudes.shape, BF16),
        ],
        scratch_shapes=[
            pltpu.SMEM(offsets.shape, jnp.int32),
            pltpu.VMEM((nblk, RIGHT_WIN, next_), BF16),
            pltpu.VMEM((nblk, LEFT_WIN, LANES), BF16),
            pltpu.SemaphoreType.DMA((2, nblk)),
            pltpu.SemaphoreType.DMA((3,)),
        ],
        compiler_params=plain,
        name="back",
    )(in_hbm(offsets), in_hbm(amplitudes), in_hbm(virtuals))

    product, slab = pl.pallas_call(
        functools.partial(ready_kernel, nblk, ext_rows),
        in_specs=[HBM, VMEM, HBM, VMEM, VMEM],
        out_specs=[VMEM] * 2,
        out_shape=[
            jax.ShapeDtypeStruct(amplitudes.shape, F32),
            jax.ShapeDtypeStruct((WIDTH, nblk * WIDTH), BF16),
        ],
        scratch_shapes=[
            pltpu.SMEM(screened.shape, jnp.int32),
            pltpu.VMEM(integrals.shape, BF16),
            pltpu.SemaphoreType.DMA((2,)),
        ],
        compiler_params=plain,
        name="ready",
    )(
        in_hbm(screened), counts[None], in_hbm(integrals), energies[None], held
    )

    stages, below = [], 1
    while below < n:
        stages.append((below, 4 if n // below % 4 == 0 else 2))
        below *= stages[-1][1]
    turned = len({radix for _, radix in stages}) == 1

    def peer(step, turn, i, h):
        below, radix = stages[(step + h * turned) % len(stages)]
        digit = i // below % radix
        return i + ((digit ^ turn) - digit) * below

    def reaches(step):
        parts = []
        for turn in range(1, stages[step][1]):
            ring = [
                (i * halves + h, peer(step, turn, i, h) * halves + h)
                for i in range(n)
                for h in range(halves)
            ]
            parts.append(lax.ppermute(partial, ("sp", "pb"), ring))
        return parts

    for step in range(len(stages) - 1):
        parts = [partial] + reaches(step)
        partial = pl.pallas_call(
            sum_kernel,
            in_specs=[VMEM] * len(parts),
            out_specs=VMEM,
            out_shape=jax.ShapeDtypeStruct(partial.shape, BF16),
            compiler_params=plain,
            name="sum",
        )(*parts)
    parts = [partial] + reaches(len(stages) - 1)
    raw = pl.pallas_call(
        functools.partial(raw_kernel, pairs),
        in_specs=[VMEM] * (1 + len(parts)),
        out_specs=VMEM,
        out_shape=jax.ShapeDtypeStruct((n * halves, pairs, WIDTH), BF16),
        scratch_shapes=[pltpu.VMEM((span // LANES, pairs * SHELL_ROW, LANES), F32)],
        compiler_params=plain,
        name="raw",
    )(slab, *parts)

    raws = lax.all_to_all(raw, ("sp", "pb"), 0, 0, tiled=True)
    return pl.pallas_call(
        functools.partial(residual_kernel, nblk, halves, chunk),
        in_specs=[VMEM] * 5,
        out_specs=HBM,
        out_shape=jax.ShapeDtypeStruct(amplitudes.shape, BF16),
        scratch_shapes=[
            pltpu.VMEM((span // LANES, pairs * SHELL_ROW, LANES), F32),
            pltpu.VMEM((pairs, ext_rows, span), BF16),
            pltpu.VMEM(amplitudes.shape, BF16),
            pltpu.SemaphoreType.DMA((pairs // chunk,)),
        ],
        compiler_params=plain,
        name="residual",
    )(raws, coupling, left, right, product)


def solution(mesh):
    return jax.shard_map(
        shards,
        mesh=mesh,
        in_specs=(
            P("pb", "sp", None),
            P(),
            P(),
            P("sp", None),
            P("sp", None),
            P("sp"),
            P(),
            P("pb", None),
        ),
        out_specs=P("pb", "sp", None),
        check_vma=False,
    )
```

```python
import functools

import jax
import jax.numpy as jnp
from jax import lax
from jax.experimental import pallas as pl
from jax.experimental.pallas import tpu as pltpu
from jax.sharding import PartitionSpec as P

SHELL_ROW = 8
SHELL_COL = 16
WIDTH = SHELL_ROW * SHELL_COL
RIGHT_WIN = 24
LEFT_WIN = 16
LANES = 128
F32 = jnp.float32
BF16 = jnp.bfloat16
VMEM = pl.BlockSpec(memory_space=pltpu.VMEM)
HBM = pl.BlockSpec(memory_space=pltpu.HBM)


def iota(shape, dim):
    return lax.broadcasted_iota(jnp.int32, shape, dim)


def split(index, size):
    return index >> (size.bit_length() - 1), index & (size - 1)


def dot(a, b):
    return jnp.dot(a, b, preferred_element_type=F32)


def dot_t(a, b):
    return lax.dot_general(a, b, (((1,), (1,)), ((), ())), preferred_element_type=F32)


def chunk_of(pairs):
    return max(c for c in (1, 5) if pairs % c == 0)


def window(low, size, nao):
    base = jnp.minimum(low & -8, nao - size)
    return pl.multiple_of(base, 8)


def picks(offs, which, first, count, shell, size, nao):
    cols = count * size
    row, col = iota((shell, cols), 0), iota((shell, cols), 1)
    parts = []
    for t in range(count):
        low = offs[which, first + t]
        delta = low - window(low, size, nao) + t * size
        parts.append(jnp.where(col == row + delta, 1.0, 0.0))
    return jnp.concatenate(parts, axis=0).astype(BF16)


def back_kernel(
    nblk, offs_in, amp, virt, out, right, left, amps,
    offs, right_win, left_win, sems, amp_sems,
):
    pairs, ext_rows, next_ = amp.shape
    nao = virt.shape[0]
    whole = nblk * SHELL_COL
    first = lax.axis_index("sp") * ext_rows
    lane_base = pl.multiple_of(first & -LANES, LANES)
    shift = first - lane_base
    offs_load = pltpu.make_async_copy(offs_in, offs, amp_sems.at[0])
    offs_load.start()
    amp_load = pltpu.make_async_copy(amp, amps, amp_sems.at[1])
    amp_load.start()
    offs_load.wait()
    rights, lefts = [], []
    for b in range(nblk):
        base = window(offs[0, b], LEFT_WIN, nao)
        lefts.append(
            pltpu.make_async_copy(
                virt.at[pl.ds(base, LEFT_WIN), pl.ds(lane_base, LANES)],
                left_win.at[b],
                sems.at[1, b],
            )
        )
        lefts[-1].start()
    for b in range(nblk):
        base = window(offs[1, b], RIGHT_WIN, nao)
        rights.append(
            pltpu.make_async_copy(
                virt.at[pl.ds(base, RIGHT_WIN), :], right_win.at[b], sems.at[0, b]
            )
        )
        rights[-1].start()

    per = LANES // SHELL_COL
    right_picks = [
        picks(offs, 1, t * per, per, SHELL_COL, RIGHT_WIN, nao)
        for t in range(whole // LANES)
    ]
    left_picks = [
        picks(offs, 0, t * per, per, SHELL_ROW, LEFT_WIN, nao) for t in range(whole // LANES)
    ]
    lane_pick = jnp.where(
        iota((ext_rows, LANES), 1) == iota((ext_rows, LANES), 0) + shift, 1.0, 0.0
    ).astype(BF16)
    for load in lefts:
        load.wait()
    left_rows = []
    for t, pick in enumerate(left_picks):
        win = left_win[t * per : (t + 1) * per].reshape(per * LEFT_WIN, LANES)
        wide = dot(pick, win).astype(BF16)
        left[t] = dot_t(lane_pick, wide).astype(BF16)
        left_rows.append(dot_t(wide, lane_pick).astype(BF16))
    for load in rights:
        load.wait()
    for t, pick in enumerate(right_picks):
        win = right_win[t * per : (t + 1) * per].reshape(per * RIGHT_WIN, next_)
        right[t * LANES : (t + 1) * LANES, :] = dot(pick, win).astype(BF16)

    amp_load.wait()
    half = dot_t(amps[...].reshape(pairs * ext_rows, next_), right[...]).astype(BF16)
    side = 2 if pairs % 2 == 0 else 1
    block_of, _ = split(iota((SHELL_ROW, side * LANES), 1) & (LANES - 1), SHELL_COL)
    for q in range(0, pairs, side):
        for t in range(whole // LANES):
            lanes = slice(t * LANES, (t + 1) * LANES)
            beside = jnp.concatenate(
                [half[(q + u) * ext_rows : (q + u + 1) * ext_rows, lanes] for u in range(side)],
                axis=1,
            )
            full = dot(left_rows[t], beside)
            kept = full[:SHELL_ROW]
            for m in range(1, per):
                kept = jnp.where(block_of == m, full[m * SHELL_ROW : (m + 1) * SHELL_ROW], kept)
            for u in range(side):
                rows = slice((q + u) * SHELL_ROW, (q + u + 1) * SHELL_ROW)
                out[rows, lanes] = kept[:, u * LANES : (u + 1) * LANES].astype(BF16)


def ready_kernel(
    nblk, ext_rows, lists_in, live, slab, energies, amps, product, slab_out, lists, slab_in, sems
):
    load = pltpu.make_async_copy(lists_in, lists, sems.at[0])
    load.start()
    slab_load = pltpu.make_async_copy(slab, slab_in, sems.at[1])
    slab_load.start()
    first = lax.axis_index("sp") * ext_rows
    lane_base = pl.multiple_of(first & -LANES, LANES)
    near = energies[:, pl.ds(lane_base, LANES)]
    own = iota((ext_rows, LANES), 1) == iota((ext_rows, LANES), 0) + (first - lane_base)
    own_e = jnp.sum(jnp.where(own, near, 0.0), axis=1, keepdims=True)
    diag = own_e + energies[...]
    for q in range(amps.shape[0]):
        product[q] = diag * amps[q].astype(F32)
    slots = lists.shape[1]
    if slots < nblk:
        slab_out[...] = jnp.zeros(slab_out.shape, BF16)
    count = live[...]
    load.wait()
    slab_load.wait()
    for k in range(slots):
        to = pl.ds(pl.multiple_of(lists[0, k] * WIDTH, WIDTH), WIDTH)
        kept = jnp.where(k < count, slab_in[:, k * WIDTH : (k + 1) * WIDTH].astype(F32), 0.0)
        slab_out[:, to] = kept.astype(BF16)


def regroup(tiles):
    per = len(tiles)
    group, _ = split(iota(tiles[0].shape, 1), SHELL_COL)
    turned = [
        [pltpu.roll(tile, turn * SHELL_COL, 1) if turn else tile for turn in range(per)]
        for tile in tiles
    ]
    pieces = []
    for m in range(per):
        piece = turned[0][-m % per]
        for i in range(1, per):
            piece = jnp.where(group == i, turned[i][(i - m) % per], piece)
        pieces.append(piece)
    return pieces


def add_up(parts):
    total = parts[0][...].astype(F32)
    for part in parts[1:]:
        total = total + part[...].astype(F32)
    return total


def sum_kernel(*refs):
    refs[-1][...] = add_up(refs[:-1]).astype(BF16)


def raw_kernel(pairs, slab, *refs):
    parts, out, ao = refs[:-2], refs[-2], refs[-1]
    total = add_up(parts)
    laid = []
    for t in range(ao.shape[0]):
        ao[t, : total.shape[0]] = total[:, t * LANES : (t + 1) * LANES]
        laid += regroup([ao[t, pl.ds(i, pairs, stride=SHELL_ROW), :] for i in range(SHELL_ROW)])
    raw = dot_t(jnp.concatenate(laid, axis=1).astype(BF16), slab[...]).astype(BF16)
    for d in range(out.shape[0]):
        out[d] = raw


def residual_kernel(
    nblk, halves, chunk, raws, coupling, left, right, product, out, mixed, upper, result, sems
):
    pairs = raws.shape[1]
    ext_rows, next_ = product.shape[1:]
    every = jnp.concatenate(
        [
            jnp.concatenate([raws[b * halves + h].astype(F32) for b in range(nblk)], axis=1)
            for h in range(halves)
        ],
        axis=0,
    ).astype(BF16)
    coupled = dot(coupling[...], every).astype(BF16).astype(F32)
    per = LANES // SHELL_COL
    for t in range(nblk // per):
        tiles = [
            coupled[:, (t * per + m) * WIDTH : (t * per + m + 1) * WIDTH] for m in range(per)
        ]
        for i, piece in enumerate(regroup(tiles)):
            mixed[t, pl.ds(i, pairs, stride=SHELL_ROW), :] = piece

    side = 2 if pairs % 2 == 0 else 1
    block_of, _ = split(iota((SHELL_ROW, side * LANES), 1) & (LANES - 1), SHELL_COL)
    for q in range(0, pairs, side):
        columns = []
        for t in range(nblk // per):
            squares = jnp.concatenate(
                [mixed[t, (q + u) * SHELL_ROW : (q + u + 1) * SHELL_ROW, :] for u in range(side)],
                axis=1,
            )
            stack = [jnp.where(block_of == m, squares, 0.0) for m in range(per)]
            columns.append(dot(left[t], jnp.concatenate(stack, axis=0).astype(BF16)))
        for u in range(side):
            lanes = slice(u * LANES, (u + 1) * LANES)
            upper[q + u] = jnp.concatenate([x[:, lanes] for x in columns], axis=1).astype(BF16)
    copies = []
    for c in range(pairs // chunk):
        part = pl.ds(c * chunk, chunk)
        flat = upper[part].reshape(chunk * ext_rows, nblk * SHELL_COL)
        inner = dot(flat, right[...]).reshape(chunk, ext_rows, next_)
        result[part] = (inner + product[part]).astype(BF16)
        copies.append(pltpu.make_async_copy(result.at[part], out.at[part], sems.at[c]))
        copies[-1].start()
    for copy in copies:
        copy.wait()


def shards(amplitudes, virtuals, energies, integrals, screened, counts, offsets, coupling):
    pairs, ext_rows, next_ = amplitudes.shape
    nblk = offsets.shape[1]
    n = lax.axis_size("sp")
    halves = lax.axis_size("pb")
    span = nblk * SHELL_COL
    chunk = chunk_of(pairs)
    strided = -(-pairs // 8) * 8 * SHELL_ROW
    plain = pltpu.CompilerParams(vmem_limit_bytes=min(60, nblk) * 1024 * 1024)
    in_hbm = functools.partial(
        pltpu.with_memory_space_constraint, memory_space=pltpu.HBM
    )

    partial, right, left, held = pl.pallas_call(
        functools.partial(back_kernel, nblk),
        in_specs=[HBM] * 3,
        out_specs=[VMEM] * 4,
        out_shape=[
            jax.ShapeDtypeStruct((pairs * SHELL_ROW, span), BF16),
            jax.ShapeDtypeStruct((span, next_), BF16),
            jax.ShapeDtypeStruct((span // LANES, ext_rows, LANES // SHELL_COL * SHELL_ROW), BF16),
            jax.ShapeDtypeStruct(amplitudes.shape, BF16),
        ],
        scratch_shapes=[
            pltpu.SMEM(offsets.shape, jnp.int32),
            pltpu.VMEM((nblk, RIGHT_WIN, next_), BF16),
            pltpu.VMEM((nblk, LEFT_WIN, LANES), BF16),
            pltpu.SemaphoreType.DMA((2, nblk)),
            pltpu.SemaphoreType.DMA((3,)),
        ],
        compiler_params=plain,
        name="back",
    )(in_hbm(offsets), in_hbm(amplitudes), in_hbm(virtuals))

    product, slab = pl.pallas_call(
        functools.partial(ready_kernel, nblk, ext_rows),
        in_specs=[HBM, VMEM, HBM, VMEM, VMEM],
        out_specs=[VMEM] * 2,
        out_shape=[
            jax.ShapeDtypeStruct(amplitudes.shape, F32),
            jax.ShapeDtypeStruct((WIDTH, nblk * WIDTH), BF16),
        ],
        scratch_shapes=[
            pltpu.SMEM(screened.shape, jnp.int32),
            pltpu.VMEM(integrals.shape, BF16),
            pltpu.SemaphoreType.DMA((2,)),
        ],
        compiler_params=plain,
        name="ready",
    )(
        in_hbm(screened), counts[None], in_hbm(integrals), energies[None], held
    )

    stages, below = [], 1
    while below < n:
        stages.append((below, 4 if n // below % 4 == 0 else 2))
        below *= stages[-1][1]
    turned = len({radix for _, radix in stages}) == 1

    def peer(step, turn, i, h):
        below, radix = stages[(step + h * turned) % len(stages)]
        digit = i // below % radix
        return i + ((digit ^ turn) - digit) * below

    def reaches(step):
        parts = []
        for turn in range(1, stages[step][1]):
            ring = [
                (i * halves + h, peer(step, turn, i, h) * halves + h)
                for i in range(n)
                for h in range(halves)
            ]
            parts.append(lax.ppermute(partial, ("sp", "pb"), ring))
        return parts

    for step in range(len(stages) - 1):
        parts = [partial] + reaches(step)
        partial = pl.pallas_call(
            sum_kernel,
            in_specs=[VMEM] * len(parts),
            out_specs=VMEM,
            out_shape=jax.ShapeDtypeStruct(partial.shape, BF16),
            compiler_params=plain,
            name="sum",
        )(*parts)
    parts = [partial] + reaches(len(stages) - 1)
    raw = pl.pallas_call(
        functools.partial(raw_kernel, pairs),
        in_specs=[VMEM] * (1 + len(parts)),
        out_specs=VMEM,
        out_shape=jax.ShapeDtypeStruct((n * halves, pairs, WIDTH), BF16),
        scratch_shapes=[pltpu.VMEM((span // LANES, strided, LANES), F32)],
        compiler_params=plain,
        name="raw",
    )(slab, *parts)

    raws = lax.all_to_all(raw, ("sp", "pb"), 0, 0, tiled=True)
    return pl.pallas_call(
        functools.partial(residual_kernel, nblk, halves, chunk),
        in_specs=[VMEM] * 5,
        out_specs=HBM,
        out_shape=jax.ShapeDtypeStruct(amplitudes.shape, BF16),
        scratch_shapes=[
            pltpu.VMEM((span // LANES, strided, LANES), F32),
            pltpu.VMEM((pairs, ext_rows, span), BF16),
            pltpu.VMEM(amplitudes.shape, BF16),
            pltpu.SemaphoreType.DMA((pairs // chunk,)),
        ],
        compiler_params=plain,
        name="residual",
    )(raws, coupling, left, right, product)


def solution(mesh):
    return jax.shard_map(
        shards,
        mesh=mesh,
        in_specs=(
            P("pb", "sp", None),
            P(),
            P(),
            P("sp", None),
            P("sp", None),
            P("sp"),
            P(),
            P("pb", None),
        ),
        out_specs=P("pb", "sp", None),
        check_vma=False,
    )
```
